512 devices in a mesh: graph: 128 (over z, y, core), sample: 4 (over x).
Axes of the slice: x: 4, y: 8, z: 8, core: 2. Of those that a mesh axis runs over, the one named last changes fastest.
Arguments:
- grid_in: bfloat16 [4, 65536, 256], P('sample', 'graph'), may hold values from -6 to 6
- mesh_init: bfloat16 [4, 16384, 512], P('sample', 'graph'), may hold values from -24 to 24
- g2m_geometry: bfloat16 [4, 131072], P(None, 'graph'), may hold values from -6 to 6
- w_embed: bfloat16 [256, 512], replicated, may hold values from -0.375 to 0.375
- w_g2m: bfloat16 [512, 512], replicated, may hold values from -0.25 to 0.25
- w_geo: bfloat16 [4, 512], replicated, may hold values from -3 to 3
- a_send: bfloat16 [512, 512], replicated, may hold values from -0.25 to 0.25
- a_recv: bfloat16 [512, 512], replicated, may hold values from -0.25 to 0.25
- b_node: bfloat16 [512, 512], replicated, may hold values from -0.25 to 0.25
- cotangent: bfloat16 [4, 16384, 512], P('sample', 'graph'), may hold values from -6 to 6
- g2m_send_rows: int32 [128, 128, 8], P('graph'), may hold values from 0 to 511
- g2m_counts: int32 [128, 128], P('graph'), may hold values from 0 to 8, as said below
- g2m_senders: int32 [131072], P('graph'), may hold values from 0 to 1023
- g2m_receivers: int32 [131072], P('graph'), may hold values from 0 to 127
- mesh_send_rows: int32 [128, 128, 4], P('graph'), may hold values from 0 to 127
- mesh_senders: int32 [65536], P('graph'), may hold values from 0 to 639
- mesh_receivers: int32 [65536], P('graph'), may hold values from 0 to 127
Outputs:
- mesh_out: bfloat16 [4, 16384, 512], P('sample', 'graph')
- grad_mesh: float32 [4, 16384, 512], P('sample', 'graph')
- grad_weights: float32 [1536, 512], P('graph')
The draws below stay inside these ranges and needn't reach their ends.
Inputs may be any that keep to these rules, and one draw needn't show every extreme that they name: `g2m_send_rows`: entry [b, g, j] is a row of band b's own 512 rows. `g2m_counts`: entry [b, g] is the number of live slots from band b to partition g; every band has some partition at 8, and some partition receives 8 from every band. `g2m_senders`: b * 8 + j names slot j from band b, for the partition that holds the edge. `g2m_receivers`: A node of the partition that holds the edge. `mesh_send_rows`: entry [b, g, j] is a row of partition b's own 128 rows. `mesh_senders`: A row of the holding partition's sender_table: below 512 a row received from another partition, else a local node. `mesh_receivers`: A node of the partition that holds the edge.
All inputs are finite; a program needn't handle non-finite values.
Results may differ from the reference program's by a relative error of at most 0.012.
The reference program's roundings to bfloat16 on the way count: a program that leaves them out, or rounds other values in their place, can miss the bound.
Values may be sent and summed in bfloat16 or wider, within the bound.
No kernel may reach another device: no remote copies, remote signals or barrier semaphores. Data moves between devices by JAX's collectives and lax.ppermute only.
A program may use at most 64 MiB of HBM per device.

```python
import jax
import jax.numpy as jnp
from jax import lax

D = 512
GI = 256
GRID_DEV = 512
MESH_DEV = 128
G2M_DEV = 1024
EDGE_DEV = 512
CAP = 8
MCAP = 4
SAMPLES = 4
GRID = 65536
MESH = 16384
G2M = 131072
EDGES = 65536
N_GRAPH = 128


def draw_g2m_counts(key, part):
    keys = jax.random.split(jax.random.fold_in(key, 17), 4)
    row_limit = jax.random.randint(keys[0], (N_GRAPH, 1), CAP // 2, CAP + 1)
    base_counts = jax.random.randint(keys[1], (N_GRAPH, N_GRAPH), 0, CAP + 1)
    counts = jnp.minimum(base_counts, row_limit)
    order = jax.random.permutation(keys[2], N_GRAPH)
    full_column = jax.random.randint(keys[3], (), 0, N_GRAPH)
    columns = jnp.arange(N_GRAPH, dtype=jnp.int32)
    counts = jnp.where(columns[None, :] == order[:, None], CAP, counts)
    counts = jnp.where(columns[None, :] == full_column, CAP, counts)
    return counts.astype(jnp.int32)


def plant(result, rng, least, top_value):
    longest = result.shape.index(max(result.shape))
    spots = []
    for shift in (0, 1):
        where = [jax.random.randint(jax.random.fold_in(rng, axis), (), 0, length) for axis, length in enumerate(result.shape)]
        where[longest] = (where[longest] + shift) % result.shape[longest]
        spots.append(tuple(where))
    return result.at[spots[0]].set(least).at[spots[1]].set(top_value)


def with_spikes(drawn, key, source, target, blocks, factor):
    owner, partner = [(jnp.arange(drawn.shape[axis_at]) // (drawn.shape[axis_at] // blocks)).reshape([-1 if axis == axis_at else 1 for axis in range(drawn.ndim)]) for axis_at in (source, target)]
    chosen = jax.random.permutation(key, blocks)[partner]
    strong = (owner == chosen) | (owner == (partner + blocks // 2) % blocks)
    return jnp.where(strong, factor * drawn, drawn)


def level_of(key, extent, shards, low, high):
    def one(position, shards_of):
        steps = jax.random.uniform(jax.random.fold_in(jax.random.fold_in(key, 6), position), (shards_of,), jnp.float32, low / len(shards), high / len(shards))
        return jnp.repeat(jnp.exp(steps), extent[position] // shards_of).reshape((-1,) + (1,) * (len(extent) - position - 1))

    level = one(*shards[0])
    for cut in shards[1:]:
        level = level * one(*cut)
    return level


def scatter_about(own_key, extent, scale, limit, cuts=(), kind=jnp.bfloat16):
    loudness = level_of(own_key, extent, cuts, -0.22, 0.18) if cuts else 1.0
    drawn = jax.random.normal(own_key, extent, jnp.float32) * scale * loudness
    return jnp.minimum(jnp.maximum(drawn, -limit), limit).astype(kind)


def gaussian_with(stream_key, extent, scale, bound, shards, heavy, kind=jnp.bfloat16):
    drawn = scale * jax.random.normal(stream_key, extent, jnp.float32)
    if shards:
        drawn = drawn * level_of(stream_key, extent, shards, -0.22, 0.18)
    return jnp.clip(with_spikes(drawn, jax.random.fold_in(stream_key, 3), *heavy), -bound, bound).astype(kind)


def setup_inputs(seed: int = 0) -> dict:
    arg_keys = jax.random.split(jax.random.key(seed), 18)
    return {
        "grid_in": scatter_about(arg_keys[0], (SAMPLES, GRID, GI), 1.0, 6.0, ((0, 4), (1, 128))),
        "mesh_init": gaussian_with(arg_keys[1], (SAMPLES, MESH, D), 1.0, 24.0, ((0, 4), (1, 128)), (1, 2, 128, 5.5)),
        "g2m_geometry": scatter_about(arg_keys[2], (4, G2M), 1.0, 6.0, ((1, 128),)),
        "w_embed": scatter_about(arg_keys[3], (GI, D), GI ** -0.5, 0.375),
        "w_g2m": scatter_about(arg_keys[4], (D, D), D ** -0.5, 0.25),
        "w_geo": scatter_about(arg_keys[5], (4, D), 4 ** -0.5, 3.0),
        "a_send": scatter_about(arg_keys[6], (D, D), D ** -0.5, 0.25),
        "a_recv": scatter_about(arg_keys[7], (D, D), D ** -0.5, 0.25),
        "b_node": scatter_about(arg_keys[8], (D, D), D ** -0.5, 0.25),
        "cotangent": scatter_about(arg_keys[9], (SAMPLES, MESH, D), 1.0, 6.0, ((0, 4), (1, 128))),
        "g2m_send_rows": plant(jax.random.randint(arg_keys[10], (N_GRAPH, N_GRAPH, CAP), 0, GRID_DEV), jax.random.fold_in(arg_keys[10], 1), 0, GRID_DEV - 1).astype(jnp.int32),
        "g2m_counts": draw_g2m_counts(jax.random.fold_in(arg_keys[17], 71), 0),
        "g2m_senders": plant(jax.random.randint(arg_keys[12], (G2M,), 0, N_GRAPH * CAP), jax.random.fold_in(arg_keys[12], 1), 0, (N_GRAPH * CAP) - 1).astype(jnp.int32),
        "g2m_receivers": plant(jax.random.randint(arg_keys[13], (G2M,), 0, MESH_DEV), jax.random.fold_in(arg_keys[13], 1), 0, MESH_DEV - 1).astype(jnp.int32),
        "mesh_send_rows": plant(jax.random.randint(arg_keys[14], (N_GRAPH, N_GRAPH, MCAP), 0, MESH_DEV), jax.random.fold_in(arg_keys[14], 1), 0, MESH_DEV - 1).astype(jnp.int32),
        "mesh_senders": plant(jax.random.randint(arg_keys[15], (EDGES,), 0, N_GRAPH * MCAP + MESH_DEV), jax.random.fold_in(arg_keys[15], 1), 0, (N_GRAPH * MCAP + MESH_DEV) - 1).astype(jnp.int32),
        "mesh_receivers": plant(jax.random.randint(arg_keys[16], (EDGES,), 0, MESH_DEV), jax.random.fold_in(arg_keys[16], 1), 0, MESH_DEV - 1).astype(jnp.int32),
    }


def silu_slope(values):
    sigmoid_v = jax.nn.sigmoid(values)
    return sigmoid_v * (1.0 + values * (1.0 - sigmoid_v))


def segment_rows(values, index_list, segments):
    moved = jnp.moveaxis(values.astype(jnp.float32), 1, 0)
    summed = jax.ops.segment_sum(moved, index_list, num_segments=segments)
    return jnp.moveaxis(summed, 0, 1)


def flat_dot(left, right):
    product = jnp.dot(left.reshape(-1, left.shape[-1]), right, preferred_element_type=jnp.float32)
    return product.reshape(left.shape[:-1] + (right.shape[-1],))


def reference(grid_in, mesh_init, g2m_geometry, w_embed, w_g2m, w_geo, a_send, a_recv, b_node, cotangent, g2m_send_rows, g2m_counts, g2m_senders, g2m_receivers, mesh_send_rows, mesh_senders, mesh_receivers):
    sources = jnp.arange(N_GRAPH, dtype=jnp.int32)
    grid_slots = jnp.arange(CAP, dtype=jnp.int32)
    local_nodes = jnp.arange(MESH_DEV, dtype=jnp.int32)
    table_size = N_GRAPH * MCAP + MESH_DEV

    def encode(device):
        picked = (sources[:, None] * GRID_DEV + g2m_send_rows[:, device, :]).reshape(-1).astype(jnp.int32)
        live_slots = (grid_slots[None, :] < g2m_counts[:, device][:, None]).reshape(-1)
        raw_rows = grid_in[:, picked, :]
        embedded = jax.nn.silu(flat_dot(raw_rows, w_embed))
        latent = jnp.where(live_slots[None, :, None], embedded, jnp.float32(0.0)).astype(jnp.bfloat16)
        grid_proj = flat_dot(latent, w_g2m)
        senders = lax.dynamic_slice_in_dim(g2m_senders, device * G2M_DEV, G2M_DEV, 0)
        receivers = lax.dynamic_slice_in_dim(g2m_receivers, device * G2M_DEV, G2M_DEV, 0)
        geometry = lax.dynamic_slice_in_dim(g2m_geometry, device * G2M_DEV, G2M_DEV, 1)
        geo_part = jnp.dot(geometry.T, w_geo, preferred_element_type=jnp.float32)
        messages = jax.nn.silu(grid_proj[:, senders, :] + geo_part[None]).astype(jnp.bfloat16)
        own_init = lax.dynamic_slice_in_dim(mesh_init, device * MESH_DEV, MESH_DEV, 1)
        return (own_init.astype(jnp.float32) + segment_rows(messages, receivers, MESH_DEV)).astype(jnp.bfloat16)

    stacked = lax.map(encode, sources)
    mesh_latent = jnp.moveaxis(stacked, 0, 1).reshape(SAMPLES, N_GRAPH * MESH_DEV, D)

    def process(carry, device):
        extra, grad_send, grad_recv, grad_node = carry
        remote_ids = (sources[:, None] * MESH_DEV + mesh_send_rows[:, device, :]).reshape(-1).astype(jnp.int32)
        node_ids = jnp.concatenate([remote_ids, (device * MESH_DEV + local_nodes).astype(jnp.int32)])
        sender_table = mesh_latent[:, node_ids, :]
        own_latent = lax.dynamic_slice_in_dim(mesh_latent, device * MESH_DEV, MESH_DEV, 1)
        senders = lax.dynamic_slice_in_dim(mesh_senders, device * EDGE_DEV, EDGE_DEV, 0)
        receivers = lax.dynamic_slice_in_dim(mesh_receivers, device * EDGE_DEV, EDGE_DEV, 0)
        send_proj = flat_dot(sender_table, a_send)
        recv_proj = flat_dot(own_latent, a_recv)
        pre_act = send_proj[:, senders, :] + recv_proj[:, receivers, :]
        edge_out = jax.nn.silu(pre_act).astype(jnp.bfloat16)
        aggregate = segment_rows(edge_out, receivers, MESH_DEV).astype(jnp.bfloat16)
        update = flat_dot(aggregate, b_node)
        mesh_new = (own_latent.astype(jnp.float32) + jax.nn.silu(update)).astype(jnp.bfloat16)
        cot_value = lax.dynamic_slice_in_dim(cotangent, device * MESH_DEV, MESH_DEV, 1).astype(jnp.float32)
        d_update = (cot_value * silu_slope(update)).astype(jnp.bfloat16)
        d_aggregate = flat_dot(d_update, b_node.T).astype(jnp.bfloat16)
        d_pre = (d_aggregate[:, receivers, :].astype(jnp.float32) * silu_slope(pre_act)).astype(jnp.bfloat16)
        recv_grad = segment_rows(d_pre, receivers, MESH_DEV).astype(jnp.bfloat16)
        send_grad = segment_rows(d_pre, senders, table_size).astype(jnp.bfloat16)
        grad_send = grad_send + jnp.dot(sender_table.reshape(-1, D).T, send_grad.reshape(-1, D), preferred_element_type=jnp.float32)
        grad_recv = grad_recv + jnp.dot(own_latent.reshape(-1, D).T, recv_grad.reshape(-1, D), preferred_element_type=jnp.float32)
        grad_node = grad_node + jnp.dot(aggregate.reshape(-1, D).T, d_update.reshape(-1, D), preferred_element_type=jnp.float32)
        returned = flat_dot(send_grad, a_send.T)
        extra = extra.at[:, node_ids, :].add(returned)
        local_grad = cot_value + flat_dot(recv_grad, a_recv.T)
        return (extra, grad_send, grad_recv, grad_node), (mesh_new, local_grad)

    start = (jnp.zeros((SAMPLES, N_GRAPH * MESH_DEV, D), jnp.float32), jnp.zeros((D, D), jnp.float32), jnp.zeros((D, D), jnp.float32), jnp.zeros((D, D), jnp.float32))
    final, outputs = lax.scan(process, start, sources)
    extra, grad_send, grad_recv, grad_node = final
    mesh_new, local_grad = outputs
    mesh_out = jnp.moveaxis(mesh_new, 0, 1).reshape(SAMPLES, N_GRAPH * MESH_DEV, D)
    grad_mesh = jnp.moveaxis(local_grad, 0, 1).reshape(SAMPLES, N_GRAPH * MESH_DEV, D) + extra
    grad_weights = jnp.concatenate([grad_send, grad_recv, grad_node], axis=0)
    return mesh_out, grad_mesh, grad_weights
```

```python
import functools

import jax
import jax.numpy as jnp
from jax import lax
from jax.experimental import pallas as pl
from jax.experimental.pallas import tpu as pltpu
from jax.sharding import Mesh
from jax.sharding import PartitionSpec as P

GRAPH = ("graph_0", "graph_1", "graph_2")
LANES = 128
F32 = jnp.float32
BF16 = jnp.bfloat16


def dot(left, right):
    return jnp.dot(left, right, preferred_element_type=F32)


def times_transposed(left, right):
    return lax.dot_general(left, right, (((1,), (1,)), ((), ())), preferred_element_type=F32)


def inner_rows(left, right):
    return lax.dot_general(left, right, (((0,), (0,)), ((), ())), preferred_element_type=F32)


def logistic(v):
    return 0.5 * jnp.tanh(0.5 * v) + 0.5


def silu(v):
    return v * logistic(v)


def slope_from(v, s):
    return s * (1.0 + v * (1.0 - s))


def columns_of(row):
    return jnp.transpose(jnp.broadcast_to(row, (LANES, row.shape[1])))


def select_rows(column, size):
    lane = lax.broadcasted_iota(jnp.int32, column.shape, 1)
    blocks = [
        jnp.where(column == lane + LANES * k, 1.0, 0.0).astype(BF16) for k in range(size // LANES)
    ]
    return blocks[0] if len(blocks) == 1 else jnp.concatenate(blocks, axis=1)


def select_columns(row, size):
    segment = lax.broadcasted_iota(jnp.int32, (size, row.shape[1]), 0)
    return jnp.where(segment == row, 1.0, 0.0).astype(BF16)


def strided_store(spread, start, stride, value):
    rows, width = value.shape
    for k in range(width // LANES):
        spread[k, pl.ds(start, rows, stride=stride), :] = value[:, k * LANES : (k + 1) * LANES]


def gather_blocks(spread, out_ref):
    for k in range(spread.shape[0]):
        out_ref[:, k * LANES : (k + 1) * LANES] = spread[k].astype(out_ref.dtype)


def scatter_blocks(spread, in_ref):
    for k in range(spread.shape[0]):
        spread[k] = in_ref[:, k * LANES : (k + 1) * LANES].astype(spread.dtype)


def pick_grid(rows_ref, counts_ref, grid_ref, out_ref, spread):
    groups, slots = rows_ref.shape[1:]
    counts = columns_of(counts_ref[...])
    wanted = rows_ref[0]
    for j in range(slots):
        row_ids = jnp.where(counts > j, wanted[:, j : j + 1], -1)
        chosen = dot(select_rows(row_ids, grid_ref.shape[1]), grid_ref[0])
        strided_store(spread, j, slots, chosen)
    gather_blocks(spread, out_ref)


def encode(
    pieces_ref, senders_ref, receivers_ref, geometry_ref, w_embed_ref, w_g2m_ref, w_geo_ref,
    init_ref, send_rows_ref, latent_ref, halo_ref, spread,
):
    edges = senders_ref.shape[1]
    nodes, width = latent_ref.shape
    step = 256
    total = init_ref[0].astype(F32)
    for start in range(0, edges, step):
        span = slice(start, start + step)
        chosen = select_rows(columns_of(senders_ref[:, span]), pieces_ref.shape[0])
        raw = dot(chosen, pieces_ref[...]).astype(BF16)
        embedded = silu(dot(raw, w_embed_ref[...])).astype(BF16)
        geo_part = inner_rows(geometry_ref[:, span], w_geo_ref[...])
        message = silu(dot(embedded, w_g2m_ref[...]) + geo_part).astype(BF16)
        total = total + dot(select_columns(receivers_ref[:, span], nodes), message)
    latent = total.astype(BF16)
    latent_ref[...] = latent
    groups, slots = send_rows_ref.shape[1:]
    wanted = send_rows_ref[0]
    for j in range(slots):
        row_ids = jnp.broadcast_to(wanted[:, j : j + 1], (groups, LANES))
        split_store(spread, j, slots, dot(select_rows(row_ids, nodes), latent))
    gather_blocks(spread, halo_ref)


def split_store(spread, j, slots, value):
    groups, width = value.shape
    strided_store(spread, j, 2 * slots, value[:, : width // 2])
    strided_store(spread, slots + j, 2 * slots, value[:, width // 2 :])


def split_load(spread, j, slots, groups):
    blocks = [
        spread[k, pl.ds(start, groups, stride=2 * slots), :]
        for start in (j, slots + j)
        for k in range(spread.shape[0])
    ]
    return jnp.concatenate(blocks, axis=1)


def process(
    slots, halo_ref, latent_ref, senders_ref, receivers_ref, a_send_ref, a_recv_ref, b_node_ref, cot_ref,
    out_ref, back_ref, table_ref, send_grad_ref, recv_grad_ref, aggregate_ref, d_update_ref, spread,
):
    nodes, width = latent_ref.shape
    rows = table_ref.shape[0]
    remote = rows - nodes
    groups = remote // slots
    scatter_blocks(spread, halo_ref)
    for j in range(slots):
        table_ref[j * groups : (j + 1) * groups, :] = split_load(spread, j, slots, groups).astype(BF16)
    latent = latent_ref[...]
    table_ref[remote:, :] = latent
    ids = senders_ref[...]
    ids = jnp.where(ids < remote, lax.rem(ids, slots) * groups + lax.div(ids, slots), ids)
    receivers = receivers_ref[...]
    receive = select_rows(columns_of(receivers), nodes)
    gather = select_columns(receivers, nodes)
    sent = dot(select_rows(columns_of(ids), rows), table_ref[...]).astype(BF16)
    own = dot(receive, latent).astype(BF16)
    pre_act = dot(sent, a_send_ref[...]) + dot(own, a_recv_ref[...])
    gate = logistic(pre_act)
    aggregate = dot(gather, (pre_act * gate).astype(BF16)).astype(BF16)
    aggregate_ref[...] = aggregate
    update = dot(aggregate, b_node_ref[...])
    update_gate = logistic(update)
    out_ref[0] = (latent.astype(F32) + update * update_gate).astype(BF16)
    d_update = (cot_ref[0].astype(F32) * slope_from(update, update_gate)).astype(BF16)
    d_update_ref[...] = d_update
    d_aggregate = times_transposed(d_update, b_node_ref[...]).astype(BF16)
    d_pre = (dot(receive, d_aggregate) * slope_from(pre_act, gate)).astype(BF16)
    recv_grad_ref[...] = dot(gather, d_pre).astype(BF16)
    send_grad = dot(select_columns(ids, rows), d_pre)
    send_grad_ref[...] = send_grad.astype(BF16)
    for j in range(slots):
        split_store(spread, j, slots, send_grad[j * groups : (j + 1) * groups])
    gather_blocks(spread, back_ref)


def weight_grads(
    half_ref, table_ref, send_grad_ref, latent_ref, recv_grad_ref, aggregate_ref, d_update_ref, out_ref
):
    half = out_ref.shape[1]
    width = latent_ref.shape[1]
    columns = pl.ds(pl.multiple_of(half_ref[0] * half, half), half)
    pairs = ((table_ref, send_grad_ref), (latent_ref, recv_grad_ref), (aggregate_ref, d_update_ref))
    for i, (left, right) in enumerate(pairs):
        product = inner_rows(left[...], right[:, columns])
        out_ref[i * width : (i + 1) * width, :] = product.astype(out_ref.dtype)


def pack(keep_ref, other_ref, back_ref, out_ref):
    half = keep_ref.shape[2]
    mid = half // 2
    tile = back_ref.shape[2]
    out_ref[:, :, :, :half] = back_ref[...]
    for i in range(3):
        rows = slice(i * tile, (i + 1) * tile)
        total = (keep_ref[:, rows, :] + other_ref[:, rows, :].astype(F32)).astype(BF16)
        if i == 1:
            out_ref[:, 0, :, 2 * half :] = total[:, :, :mid]
            out_ref[:, 1, :, 2 * half :] = total[:, :, mid:]
        else:
            out_ref[:, i // 2, :, half : 2 * half] = total


def add_chips(arrived_ref, out_ref):
    chips = arrived_ref.shape[0]
    skip = arrived_ref.shape[3] - out_ref.shape[3]
    total = arrived_ref[0, :, :, skip:].astype(F32)
    for i in range(1, chips):
        total = total + arrived_ref[i, :, :, skip:].astype(F32)
    for i in range(out_ref.shape[0]):
        out_ref[i] = total


def add_samples(core_ref, arrived_ref, out_ref):
    samples, _, _, tile, lanes = arrived_ref.shape
    half = out_ref.shape[1] // 2
    mid = half // 2
    total = arrived_ref[0]
    for i in range(1, samples):
        total = total + arrived_ref[i]
    extra = tile // 2

    def middle(rows):
        parts = [total[core, h, rows, half:] for h in range(2) for core in range(2)]
        return jnp.concatenate(parts, axis=1)

    def whole(core):
        return jnp.concatenate([total[core, h, :, :half] for h in range(2)], axis=1)

    @pl.when(core_ref[0] == 0)
    def _():
        out_ref[:tile, :] = whole(0)
        out_ref[tile:, :] = middle(slice(0, extra))

    @pl.when(core_ref[0] == 1)
    def _():
        out_ref[:extra, :] = middle(slice(extra, tile))
        out_ref[extra:, :] = whole(1)


def return_grads(
    back_ref, send_rows_ref, send_grad_ref, recv_grad_ref, a_send_ref, a_recv_ref, cot_ref,
    out_ref, spread,
):
    nodes = recv_grad_ref.shape[0]
    groups, slots = send_rows_ref.shape[1:]
    scatter_blocks(spread, back_ref)
    total = send_grad_ref[...].astype(F32)
    wanted = send_rows_ref[0]
    for j in range(slots):
        row_ids = jnp.broadcast_to(wanted[:, j : j + 1], (groups, LANES))
        arrived = split_load(spread, j, slots, groups).astype(BF16)
        total = total + inner_rows(select_rows(row_ids, nodes), arrived)
    high = total.astype(BF16)
    rest = total - high.astype(F32)
    low = rest.astype(BF16)
    a_send = a_send_ref[...]
    out_ref[0] = (
        cot_ref[0].astype(F32)
        + times_transposed(recv_grad_ref[...], a_recv_ref[...])
        + (times_transposed(high, a_send) + times_transposed(low, a_send))
    )


def shape(dims, dtype):
    return jax.ShapeDtypeStruct(dims, dtype)


def kernel(body, outs, scratch, flops, smem_first=False):
    def call(*operands):
        specs = [pl.BlockSpec(memory_space=pltpu.VMEM) for _ in operands]
        if smem_first:
            specs[0] = pl.BlockSpec(memory_space=pltpu.SMEM)
        moved = sum(x.size * x.dtype.itemsize for x in operands)
        return pl.pallas_call(
            body,
            out_shape=outs,
            in_specs=specs,
            out_specs=jax.tree.map(lambda _: pl.BlockSpec(memory_space=pltpu.VMEM), outs),
            scratch_shapes=scratch,
            compiler_params=pltpu.CompilerParams(vmem_limit_bytes=24 << 20),
            cost_estimate=pl.CostEstimate(flops=flops, bytes_accessed=moved, transcendentals=0),
        )(*operands)

    return call


def exchange(x, axis):
    return lax.all_to_all(x, axis, split_axis=0, concat_axis=0, tiled=True)


def share(keep, send, back, core):
    half = keep.shape[1]
    tile = 8
    chips = lax.axis_size("graph_0") * lax.axis_size("graph_1")
    samples = lax.axis_size("sample")
    lanes = 2 * half + half // 2
    other = lax.ppermute(send, "graph_2", [(0, 1), (1, 0)])
    packed = kernel(pack, shape((chips, 2, tile, lanes), BF16), [], 10**7)(
        keep.reshape(chips, -1, half),
        other.reshape(chips, -1, half),
        back.reshape(chips, 2, tile, half),
    )
    arrived = exchange(packed.reshape(2 * chips, tile, lanes), GRAPH)
    copies = kernel(add_chips, shape((2 * samples, 2, tile, lanes - half), F32), [], 10**7)(
        arrived.reshape(chips, 2, tile, lanes)
    )
    copies = exchange(copies, ("sample", "graph_2"))
    rows = keep.shape[0] // (2 * chips)
    grad_weights = kernel(add_samples, shape((rows, 2 * half), F32), [], 10**6, True)(
        core, copies.reshape(samples, 2, 2, tile, lanes - half)
    )
    return arrived.reshape(2 * chips * tile, lanes), grad_weights


def on_device(
    grid_in,
    mesh_init,
    g2m_geometry,
    w_embed,
    w_g2m,
    w_geo,
    a_send,
    a_recv,
    b_node,
    cotangent,
    g2m_send_rows,
    g2m_counts,
    g2m_senders,
    g2m_receivers,
    mesh_send_rows,
    mesh_senders,
    mesh_receivers,
):
    groups, slots = g2m_send_rows.shape[1:]
    halo_slots = mesh_send_rows.shape[2]
    features = grid_in.shape[2]
    width = w_g2m.shape[1]
    half = width // 2
    nodes = mesh_init.shape[1]
    table_rows = groups * halo_slots + nodes
    halves = 2 * groups * halo_slots

    raw_rows = kernel(
        pick_grid,
        shape((groups * slots, features), BF16),
        [pltpu.VMEM((features // LANES, groups * slots, LANES), F32)],
        10**8,
    )(g2m_send_rows, g2m_counts, grid_in)
    pieces = exchange(raw_rows.reshape(groups, slots, features), GRAPH)

    latent, halo = kernel(
        encode,
        (shape((nodes, width), BF16), shape((halves, half), BF16)),
        [pltpu.VMEM((half // LANES, halves, LANES), F32)],
        2 * 10**9,
    )(
        pieces.reshape(groups * slots, features),
        g2m_senders[None],
        g2m_receivers[None],
        g2m_geometry,
        w_embed,
        w_g2m,
        w_geo,
        mesh_init,
        mesh_send_rows,
    )
    halo = exchange(halo.reshape(groups, 2 * halo_slots, half), GRAPH)

    mesh_out, back, table, send_grad, recv_grad, aggregate, d_update = kernel(
        functools.partial(process, halo_slots),
        (
            shape((1, nodes, width), BF16),
            shape((halves, half), BF16),
            shape((table_rows, width), BF16),
            shape((table_rows, width), BF16),
            shape((nodes, width), BF16),
            shape((nodes, width), BF16),
            shape((nodes, width), BF16),
        ),
        [pltpu.VMEM((half // LANES, halves, LANES), F32)],
        3 * 10**9,
    )(
        halo.reshape(halves, half),
        latent,
        mesh_senders[None],
        mesh_receivers[None],
        a_send,
        a_recv,
        b_node,
        cotangent,
    )
    core = lax.axis_index("graph_2").astype(jnp.int32)[None]
    operands = (table, send_grad, latent, recv_grad, aggregate, d_update)
    send = kernel(weight_grads, shape((3 * width, half), BF16), [], 5 * 10**8, True)(1 - core, *operands)
    keep = kernel(weight_grads, shape((3 * width, half), F32), [], 5 * 10**8, True)(core, *operands)
    arrived, grad_weights = share(keep, send, back, core)

    grad_mesh = kernel(
        return_grads,
        shape((1, nodes, width), F32),
        [pltpu.VMEM((half // LANES, halves, LANES), F32)],
        10**9,
    )(
        arrived,
        mesh_send_rows,
        send_grad[groups * halo_slots :],
        recv_grad,
        a_send,
        a_recv,
        cotangent,
    )
    return (mesh_out, grad_mesh, grad_weights)


def solution(mesh):
    torus = Mesh(
        mesh.devices.reshape(8, 8, 2, mesh.shape["sample"]),
        ("graph_0", "graph_1", "graph_2", "sample"),
    )
    in_specs = (
        P("sample", GRAPH, None),
        P("sample", GRAPH, None),
        P(None, GRAPH),
        P(),
        P(),
        P(),
        P(),
        P(),
        P(),
        P("sample", GRAPH, None),
        P(GRAPH, None, None),
        P(GRAPH, None),
        P(GRAPH),
        P(GRAPH),
        P(GRAPH, None, None),
        P(GRAPH),
        P(GRAPH),
    )
    out_specs = (P("sample", GRAPH, None), P("sample", GRAPH, None), P(GRAPH, None))
    return jax.shard_map(
        on_device, mesh=torus, in_specs=in_specs, out_specs=out_specs, check_vma=False
    )
```

```python
import functools

import jax
import jax.numpy as jnp
from jax import lax
from jax.experimental import pallas as pl
from jax.experimental.pallas import tpu as pltpu
from jax.sharding import Mesh
from jax.sharding import PartitionSpec as P

GRAPH = ("graph_0", "graph_1", "graph_2")
LANES = 128
F32 = jnp.float32
BF16 = jnp.bfloat16
GRANTS = (60, 40, 40)


def dot(left, right):
    return jnp.dot(left, right, preferred_element_type=F32)


def times_transposed(left, right):
    return lax.dot_general(left, right, (((1,), (1,)), ((), ())), preferred_element_type=F32)


def inner_rows(left, right):
    return lax.dot_general(left, right, (((0,), (0,)), ((), ())), preferred_element_type=F32)


def logistic(v):
    return 0.5 * jnp.tanh(0.5 * v) + 0.5


def silu(v):
    return v * logistic(v)


def slope_from(v, s):
    return s * (1.0 + v * (1.0 - s))


def columns_of(row):
    return jnp.transpose(jnp.broadcast_to(row, (LANES, row.shape[1])))


def slot_columns(ids):
    slots, groups = ids.shape
    turned = jnp.transpose(jnp.concatenate([ids] * (LANES // slots), axis=0))
    return [jnp.broadcast_to(turned[:, j : j + 1], (groups, LANES)) for j in range(slots)]


def select_rows(column, size):
    lane = lax.broadcasted_iota(jnp.int32, column.shape, 1)
    blocks = [
        jnp.where(column == lane + LANES * k, 1.0, 0.0).astype(BF16) for k in range(size // LANES)
    ]
    return blocks[0] if len(blocks) == 1 else jnp.concatenate(blocks, axis=1)


def select_columns(row, size):
    segment = lax.broadcasted_iota(jnp.int32, (size, row.shape[1]), 0)
    return jnp.where(segment == row, 1.0, 0.0).astype(BF16)


def strided_store(spread, start, stride, value):
    rows, width = value.shape
    for k in range(width // LANES):
        spread[k, pl.ds(start, rows, stride=stride), :] = value[:, k * LANES : (k + 1) * LANES]


def gather_blocks(spread, out_ref):
    for k in range(spread.shape[0]):
        out_ref[:, k * LANES : (k + 1) * LANES] = spread[k].astype(out_ref.dtype)


def scatter_blocks(spread, in_ref):
    for k in range(spread.shape[0]):
        spread[k] = in_ref[:, k * LANES : (k + 1) * LANES].astype(spread.dtype)


def pick_grid(rows_hbm, counts_hbm, grid_hbm, out_ref, rows, counts, grid, sems, spread):
    copies = [
        pltpu.make_async_copy(source, target, sems.at[i])
        for i, (source, target) in enumerate(
            ((rows_hbm, rows), (counts_hbm, counts), (grid_hbm, grid))
        )
    ]
    for copy in copies:
        copy.start()
    copies[0].wait()
    copies[1].wait()
    slots = rows.shape[1]
    slot = lax.broadcasted_iota(jnp.int32, rows.shape[1:], 0)
    ids = slot_columns(jnp.where(slot < counts[...], rows[0], -1))
    chosen = [select_rows(ids[j], grid.shape[1]) for j in range(slots)]
    copies[2].wait()
    for j in range(slots):
        strided_store(spread, j, slots, dot(chosen[j], grid[0]))
    gather_blocks(spread, out_ref)


def encode(
    pieces_ref, senders_ref, receivers_ref, geometry_ref, w_embed_ref, w_g2m_ref, w_geo_ref,
    init_ref, send_rows_ref, latent_ref, halo_ref, spread,
):
    edges = senders_ref.shape[1]
    nodes, width = latent_ref.shape
    step = 256
    total = init_ref[0].astype(F32)
    for start in range(0, edges, step):
        span = slice(start, start + step)
        chosen = select_rows(columns_of(senders_ref[:, span]), pieces_ref.shape[0])
        raw = dot(chosen, pieces_ref[...]).astype(BF16)
        embedded = silu(dot(raw, w_embed_ref[...])).astype(BF16)
        geo_part = inner_rows(geometry_ref[:, span], w_geo_ref[...])
        message = silu(dot(embedded, w_g2m_ref[...]) + geo_part).astype(BF16)
        total = total + dot(select_columns(receivers_ref[:, span], nodes), message)
    latent = total.astype(BF16)
    latent_ref[...] = latent
    ids = slot_columns(send_rows_ref[0])
    for j in range(len(ids)):
        split_store(spread, j, len(ids), dot(select_rows(ids[j], nodes), latent))
    gather_blocks(spread, halo_ref)


def split_store(spread, j, slots, value):
    groups, width = value.shape
    strided_store(spread, j, 2 * slots, value[:, : width // 2])
    strided_store(spread, slots + j, 2 * slots, value[:, width // 2 :])


def split_load(spread, j, slots, groups):
    blocks = [
        spread[k, pl.ds(start, groups, stride=2 * slots), :]
        for start in (j, slots + j)
        for k in range(spread.shape[0])
    ]
    return jnp.concatenate(blocks, axis=1)


def process(
    slots, halo_ref, latent_ref, senders_ref, receivers_ref, a_send_ref, a_recv_ref, b_node_ref,
    cot_ref,
    out_ref, back_ref, table_ref, send_grad_ref, recv_grad_ref, aggregate_ref, d_update_ref, spread,
):
    nodes, width = latent_ref.shape
    rows = table_ref.shape[0]
    remote = rows - nodes
    groups = remote // slots
    scatter_blocks(spread, halo_ref)
    for j in range(slots):
        table_ref[j * groups : (j + 1) * groups, :] = split_load(spread, j, slots, groups).astype(BF16)
    latent = latent_ref[...]
    table_ref[remote:, :] = latent
    ids = senders_ref[...]
    ids = jnp.where(ids < remote, lax.rem(ids, slots) * groups + lax.div(ids, slots), ids)
    receivers = receivers_ref[...]
    receive = select_rows(columns_of(receivers), nodes)
    gather = select_columns(receivers, nodes)
    sent = dot(select_rows(columns_of(ids), rows), table_ref[...]).astype(BF16)
    own = dot(receive, latent).astype(BF16)
    pre_act = dot(sent, a_send_ref[...]) + dot(own, a_recv_ref[...])
    gate = logistic(pre_act)
    aggregate = dot(gather, (pre_act * gate).astype(BF16)).astype(BF16)
    aggregate_ref[...] = aggregate
    update = dot(aggregate, b_node_ref[...])
    update_gate = logistic(update)
    out_ref[0] = (latent.astype(F32) + update * update_gate).astype(BF16)
    d_update = (cot_ref[0].astype(F32) * slope_from(update, update_gate)).astype(BF16)
    d_update_ref[...] = d_update
    d_aggregate = times_transposed(d_update, b_node_ref[...]).astype(BF16)
    d_pre = (dot(receive, d_aggregate) * slope_from(pre_act, gate)).astype(BF16)
    recv_grad_ref[...] = dot(gather, d_pre).astype(BF16)
    send_grad = dot(select_columns(ids, rows), d_pre)
    send_grad_ref[...] = send_grad.astype(BF16)
    for j in range(slots):
        split_store(spread, j, slots, send_grad[j * groups : (j + 1) * groups])
    gather_blocks(spread, back_ref)


def weight_grads(
    half_ref, table_ref, send_grad_ref, latent_ref, recv_grad_ref, aggregate_ref, d_update_ref, out_ref
):
    half = out_ref.shape[1]
    width = latent_ref.shape[1]
    columns = pl.ds(pl.multiple_of(half_ref[0] * half, half), half)
    pairs = ((table_ref, send_grad_ref), (latent_ref, recv_grad_ref), (aggregate_ref, d_update_ref))
    for i, (left, right) in enumerate(pairs):
        product = inner_rows(left[...], right[:, columns])
        out_ref[i * width : (i + 1) * width, :] = product.astype(out_ref.dtype)


def pack(keep_ref, other_ref, back_ref, out_ref):
    chips, _, half = keep_ref.shape
    tile = back_ref.shape[2]
    out_ref[:, :, :, :half] = back_ref[...]
    for i in range(3):
        rows = slice(i * tile, (i + 1) * tile)
        total = keep_ref[:, rows, :] + other_ref[:, rows, :].astype(F32)
        if i != 1:
            out_ref[:, i // 2, :, half : 2 * half] = total.astype(BF16)
            continue
        flat = total.reshape(chips * tile, half)
        left, right = flat[:, :LANES], flat[:, LANES:]
        upper = lax.rem(lax.broadcasted_iota(jnp.int32, left.shape, 0), tile) < tile // 2
        first = jnp.where(upper, left, pltpu.roll(right, tile // 2, 0))
        second = jnp.where(upper, pltpu.roll(left, chips * tile - tile // 2, 0), right)
        out_ref[:, 0, :, 2 * half :] = first.astype(BF16).reshape(chips, tile, LANES)
        out_ref[:, 1, :, 2 * half :] = second.astype(BF16).reshape(chips, tile, LANES)


def add_chips(arrived_ref, out_ref):
    chips = arrived_ref.shape[0]
    skip = arrived_ref.shape[3] - out_ref.shape[2]
    total = arrived_ref[0, :, :, skip:].astype(F32)
    for i in range(1, chips):
        total = total + arrived_ref[i, :, :, skip:].astype(F32)
    out_ref[...] = total


def add_samples(core_ref, own_ref, next_ref, across_ref, last_ref, out_ref):
    total = (own_ref[...] + across_ref[...]) + (next_ref[...] + last_ref[...])
    tile = total.shape[1]
    half = out_ref.shape[1] // 2
    extra = tile // 2
    whole = jnp.concatenate([total[h, :, :half] for h in range(2)], axis=1)
    parts = [total[h, k * extra : (k + 1) * extra, half:] for h in range(2) for k in range(2)]
    middle = jnp.concatenate(parts, axis=1)

    @pl.when(core_ref[0] == 0)
    def _():
        out_ref[:tile, :] = whole
        out_ref[tile:, :] = middle

    @pl.when(core_ref[0] == 1)
    def _():
        out_ref[:extra, :] = middle
        out_ref[extra:, :] = whole


def return_grads(
    back_ref, send_rows_ref, send_grad_ref, recv_grad_ref, a_send_ref, a_recv_ref, cot_ref,
    out_ref, spread,
):
    nodes = recv_grad_ref.shape[0]
    slots, groups = send_rows_ref.shape[1:]
    scatter_blocks(spread, back_ref)
    total = send_grad_ref[...].astype(F32)
    wanted = send_rows_ref[0]
    for j in range(slots):
        arrived = split_load(spread, j, slots, groups).astype(BF16)
        total = total + dot(select_columns(wanted[j : j + 1], nodes), arrived)
    high = total.astype(BF16)
    rest = total - high.astype(F32)
    low = rest.astype(BF16)
    a_send = a_send_ref[...]
    out_ref[0] = (
        cot_ref[0].astype(F32)
        + times_transposed(recv_grad_ref[...], a_recv_ref[...])
        + (times_transposed(high, a_send) + times_transposed(low, a_send))
    )


def shape(dims, dtype):
    return jax.ShapeDtypeStruct(dims, dtype)


def kernel(body, outs, scratch, flops, first=0, space=None, grant=24):
    def call(*operands):
        specs = [
            pl.BlockSpec(memory_space=space if i < first else pltpu.VMEM)
            for i in range(len(operands))
        ]
        moved = sum(x.size * x.dtype.itemsize for x in operands)
        return pl.pallas_call(
            body,
            out_shape=outs,
            in_specs=specs,
            out_specs=jax.tree.map(lambda _: pl.BlockSpec(memory_space=pltpu.VMEM), outs),
            scratch_shapes=scratch,
            compiler_params=pltpu.CompilerParams(vmem_limit_bytes=grant << 20),
            cost_estimate=pl.CostEstimate(flops=flops, bytes_accessed=moved, transcendentals=0),
        )(*operands)

    return call


def exchange(x, axis):
    return lax.all_to_all(x, axis, split_axis=0, concat_axis=0, tiled=True)


def share(keep, send, back, core):
    half = keep.shape[1]
    tile = 8
    chips = lax.axis_size("graph_0") * lax.axis_size("graph_1")
    samples = lax.axis_size("sample")
    lanes = 2 * half + half // 2
    other = lax.ppermute(send, "graph_2", [(0, 1), (1, 0)])
    packed = kernel(pack, shape((chips, 2, tile, lanes), BF16), [], 10**7)(
        keep.reshape(chips, -1, half),
        other.reshape(chips, -1, half),
        back.reshape(chips, 2, tile, half),
    )
    arrived = exchange(packed.reshape(2 * chips, tile, lanes), GRAPH)
    own = kernel(add_chips, shape((2, tile, lanes - half), F32), [], 10**7)(
        arrived.reshape(chips, 2, tile, lanes)
    )
    others = [
        lax.ppermute(own, "sample", [((i + step) % samples, i) for i in range(samples)])
        for step in range(1, samples)
    ]
    rows = keep.shape[0] // (2 * chips)
    grad_weights = kernel(add_samples, shape((rows, 2 * half), F32), [], 10**6, 1, pltpu.SMEM)(
        core, own, *others
    )
    return arrived.reshape(2 * chips * tile, lanes), grad_weights


def on_device(
    grid_in,
    mesh_init,
    g2m_geometry,
    w_embed,
    w_g2m,
    w_geo,
    a_send,
    a_recv,
    b_node,
    cotangent,
    g2m_send_rows,
    g2m_counts,
    g2m_senders,
    g2m_receivers,
    mesh_send_rows,
    mesh_senders,
    mesh_receivers,
):
    groups, slots = g2m_send_rows.shape[1:]
    halo_slots = mesh_send_rows.shape[2]
    features = grid_in.shape[2]
    width = w_g2m.shape[1]
    half = width // 2
    nodes = mesh_init.shape[1]
    table_rows = groups * halo_slots + nodes
    halves = 2 * groups * halo_slots

    grid_rows = jnp.transpose(g2m_send_rows, (0, 2, 1))
    mesh_rows = jnp.transpose(mesh_send_rows, (0, 2, 1))
    raw_rows = kernel(
        pick_grid,
        shape((groups * slots, features), BF16),
        [
            pltpu.VMEM(grid_rows.shape, jnp.int32),
            pltpu.VMEM(g2m_counts.shape, jnp.int32),
            pltpu.VMEM(grid_in.shape, BF16),
            pltpu.SemaphoreType.DMA((3,)),
            pltpu.VMEM((features // LANES, groups * slots, LANES), F32),
        ],
        10**8,
        3,
        pltpu.HBM,
        GRANTS[0],
    )(grid_rows, g2m_counts, grid_in)
    pieces = exchange(raw_rows.reshape(groups, slots, features), GRAPH)

    latent, halo = kernel(
        encode,
        (shape((nodes, width), BF16), shape((halves, half), BF16)),
        [pltpu.VMEM((half // LANES, halves, LANES), F32)],
        2 * 10**9,
        grant=GRANTS[1],
    )(
        pieces.reshape(groups * slots, features),
        g2m_senders[None],
        g2m_receivers[None],
        g2m_geometry,
        w_embed,
        w_g2m,
        w_geo,
        mesh_init,
        mesh_rows,
    )
    halo = exchange(halo.reshape(groups, 2 * halo_slots, half), GRAPH)

    mesh_out, back, table, send_grad, recv_grad, aggregate, d_update = kernel(
        functools.partial(process, halo_slots),
        (
            shape((1, nodes, width), BF16),
            shape((halves, half), BF16),
            shape((table_rows, width), BF16),
            shape((table_rows, width), BF16),
            shape((nodes, width), BF16),
            shape((nodes, width), BF16),
            shape((nodes, width), BF16),
        ),
        [pltpu.VMEM((half // LANES, halves, LANES), F32)],
        3 * 10**9,
        grant=GRANTS[2],
    )(
        halo.reshape(halves, half),
        latent,
        mesh_senders[None],
        mesh_receivers[None],
        a_send,
        a_recv,
        b_node,
        cotangent,
    )

    core = lax.axis_index("graph_2").astype(jnp.int32)[None]
    operands = (table, send_grad, latent, recv_grad, aggregate, d_update)
    send = kernel(weight_grads, shape((3 * width, half), BF16), [], 5 * 10**8, 1, pltpu.SMEM)(1 - core, *operands)
    keep = kernel(weight_grads, shape((3 * width, half), F32), [], 5 * 10**8, 1, pltpu.SMEM)(core, *operands)
    arrived, grad_weights = share(keep, send, back, core)

    grad_mesh = kernel(
        return_grads,
        shape((1, nodes, width), F32),
        [pltpu.VMEM((half // LANES, halves, LANES), F32)],
        10**9,
    )(
        arrived,
        mesh_rows,
        send_grad[groups * halo_slots :],
        recv_grad,
        a_send,
        a_recv,
        cotangent,
    )
    return (mesh_out, grad_mesh, grad_weights)


def solution(mesh):
    torus = Mesh(
        mesh.devices.reshape(8, 8, 2, mesh.shape["sample"]),
        ("graph_0", "graph_1", "graph_2", "sample"),
    )
    in_specs = (
        P("sample", GRAPH, None),
        P("sample", GRAPH, None),
        P(None, GRAPH),
        P(),
        P(),
        P(),
        P(),
        P(),
        P(),
        P("sample", GRAPH, None),
        P(GRAPH, None, None),
        P(GRAPH, None),
        P(GRAPH),
        P(GRAPH),
        P(GRAPH, None, None),
        P(GRAPH),
        P(GRAPH),
    )
    out_specs = (P("sample", GRAPH, None), P("sample", GRAPH, None), P(GRAPH, None))
    return jax.shard_map(
        on_device, mesh=torus, in_specs=in_specs, out_specs=out_specs, check_vma=False
    )
```

```python
import functools

import jax
import jax.numpy as jnp
from jax import lax
from jax.experimental import pallas as pl
from jax.experimental.pallas import tpu as pltpu
from jax.sharding import Mesh
from jax.sharding import PartitionSpec as P

GRAPH = ("graph_0", "graph_1", "graph_2")
LANES = 128
F32 = jnp.float32
BF16 = jnp.bfloat16
GRANTS = (60, 40, 40)


def dot(left, right):
    return jnp.dot(left, right, preferred_element_type=F32)


def times_transposed(left, right):
    return lax.dot_general(left, right, (((1,), (1,)), ((), ())), preferred_element_type=F32)


def inner_rows(left, right):
    return lax.dot_general(left, right, (((0,), (0,)), ((), ())), preferred_element_type=F32)


def logistic(v):
    return 0.5 * jnp.tanh(0.5 * v) + 0.5


def silu(v):
    return v * logistic(v)


def slope_from(v, s):
    return s * (1.0 + v * (1.0 - s))


def columns_of(row):
    return jnp.transpose(jnp.broadcast_to(row, (LANES, row.shape[1])))


def slot_columns(ids):
    slots, groups = ids.shape
    turned = jnp.transpose(jnp.concatenate([ids] * (LANES // slots), axis=0))
    return [jnp.broadcast_to(turned[:, j : j + 1], (groups, LANES)) for j in range(slots)]


def select_rows(column, size):
    lane = lax.broadcasted_iota(jnp.int32, column.shape, 1)
    blocks = [
        jnp.where(column == lane + LANES * k, 1.0, 0.0).astype(BF16) for k in range(size // LANES)
    ]
    return blocks[0] if len(blocks) == 1 else jnp.concatenate(blocks, axis=1)


def select_columns(row, size):
    segment = lax.broadcasted_iota(jnp.int32, (size, row.shape[1]), 0)
    return jnp.where(segment == row, 1.0, 0.0).astype(BF16)


def strided_store(spread, start, stride, value):
    rows, width = value.shape
    for k in range(width // LANES):
        spread[k, pl.ds(start, rows, stride=stride), :] = value[:, k * LANES : (k + 1) * LANES]


def gather_blocks(spread, out_ref):
    for k in range(spread.shape[0]):
        out_ref[:, k * LANES : (k + 1) * LANES] = spread[k].astype(out_ref.dtype)


def scatter_blocks(spread, in_ref):
    for k in range(spread.shape[0]):
        spread[k] = in_ref[:, k * LANES : (k + 1) * LANES].astype(spread.dtype)


def pick_grid(rows_hbm, counts_hbm, grid_hbm, out_ref, rows, counts, grid, sems, spread):
    copies = [
        pltpu.make_async_copy(source, target, sems.at[i])
        for i, (source, target) in enumerate(
            ((rows_hbm, rows), (counts_hbm, counts), (grid_hbm, grid))
        )
    ]
    for copy in copies:
        copy.start()
    copies[0].wait()
    copies[1].wait()
    slots = rows.shape[1]
    slot = lax.broadcasted_iota(jnp.int32, rows.shape[1:], 0)
    ids = slot_columns(jnp.where(slot < counts[...], rows[0], -1))
    chosen = [select_rows(ids[j], grid.shape[1]) for j in range(slots)]
    copies[2].wait()
    for j in range(slots):
        strided_store(spread, j, slots, dot(chosen[j], grid[0]))
    gather_blocks(spread, out_ref)


def encode(
    pieces_ref, senders_ref, receivers_ref, geometry_ref, w_embed_ref, w_g2m_ref, w_geo_ref,
    init_ref, send_rows_ref, latent_ref, halo_ref, spread,
):
    edges = senders_ref.shape[1]
    nodes, width = latent_ref.shape
    inputs = geometry_ref.shape[0]
    geometry = geometry_ref[...].astype(F32)
    blank = jnp.zeros((LANES - inputs, edges), F32)
    geometry = jnp.transpose(jnp.concatenate([geometry, blank], axis=0)).astype(BF16)
    blank = jnp.zeros((LANES - inputs, width), F32)
    weights = [w_g2m_ref[...].astype(F32), w_geo_ref[...].astype(F32), blank]
    weights = jnp.concatenate(weights, axis=0).astype(BF16)
    chosen = select_rows(columns_of(senders_ref[...]), pieces_ref.shape[0])
    raw = dot(chosen, pieces_ref[...]).astype(BF16)
    embedded = silu(dot(raw, w_embed_ref[...])).astype(BF16)
    message = silu(dot(jnp.concatenate([embedded, geometry], axis=1), weights)).astype(BF16)
    gather = select_columns(receivers_ref[...], nodes)
    total = init_ref[0].astype(F32) + dot(gather, message)
    latent = total.astype(BF16)
    latent_ref[...] = latent
    ids = slot_columns(send_rows_ref[0])
    for j in range(len(ids)):
        split_store(spread, j, len(ids), dot(select_rows(ids[j], nodes), latent))
    gather_blocks(spread, halo_ref)


def split_store(spread, j, slots, value):
    groups, width = value.shape
    strided_store(spread, j, 2 * slots, value[:, : width // 2])
    strided_store(spread, slots + j, 2 * slots, value[:, width // 2 :])


def split_load(spread, j, slots, groups):
    blocks = [
        spread[k, pl.ds(start, groups, stride=2 * slots), :]
        for start in (j, slots + j)
        for k in range(spread.shape[0])
    ]
    return jnp.concatenate(blocks, axis=1)


def process(
    slots, halo_ref, latent_ref, senders_ref, receivers_ref, a_send_ref, a_recv_ref, b_node_ref,
    cot_ref,
    out_ref, back_ref, table_ref, send_grad_ref, recv_grad_ref, aggregate_ref, d_update_ref, spread,
):
    nodes, width = latent_ref.shape
    rows = table_ref.shape[0]
    remote = rows - nodes
    groups = remote // slots
    scatter_blocks(spread, halo_ref)
    for j in range(slots):
        table_ref[j * groups : (j + 1) * groups, :] = split_load(spread, j, slots, groups).astype(BF16)
    latent = latent_ref[...]
    table_ref[remote:, :] = latent
    ids = senders_ref[...]
    ids = jnp.where(ids < remote, lax.rem(ids, slots) * groups + lax.div(ids, slots), ids)
    receivers = receivers_ref[...]
    receive = select_rows(columns_of(receivers), nodes)
    gather = select_columns(receivers, nodes)
    sent = dot(select_rows(columns_of(ids), rows), table_ref[...]).astype(BF16)
    own = dot(receive, latent).astype(BF16)
    pre_act = dot(sent, a_send_ref[...]) + dot(own, a_recv_ref[...])
    gate = logistic(pre_act)
    aggregate = dot(gather, (pre_act * gate).astype(BF16)).astype(BF16)
    aggregate_ref[...] = aggregate
    update = dot(aggregate, b_node_ref[...])
    update_gate = logistic(update)
    out_ref[0] = (latent.astype(F32) + update * update_gate).astype(BF16)
    d_update = (cot_ref[0].astype(F32) * slope_from(update, update_gate)).astype(BF16)
    d_update_ref[...] = d_update
    d_aggregate = times_transposed(d_update, b_node_ref[...]).astype(BF16)
    d_pre = (dot(receive, d_aggregate) * slope_from(pre_act, gate)).astype(BF16)
    recv_grad_ref[...] = dot(gather, d_pre).astype(BF16)
    send_grad = dot(select_columns(ids, rows), d_pre)
    send_grad_ref[...] = send_grad.astype(BF16)
    for j in range(slots):
        split_store(spread, j, slots, send_grad[j * groups : (j + 1) * groups])
    gather_blocks(spread, back_ref)


def weight_grads(
    mine, sibling_ref, table_ref, send_grad_ref, latent_ref, recv_grad_ref, aggregate_ref, d_update_ref, out_ref
):
    half = out_ref.shape[1]
    width = latent_ref.shape[1]
    core = 1 - sibling_ref[0] if mine else sibling_ref[0]
    columns = pl.ds(pl.multiple_of(core * half, half), half)
    pairs = ((table_ref, send_grad_ref), (latent_ref, recv_grad_ref), (aggregate_ref, d_update_ref))
    for i, (left, right) in enumerate(pairs):
        product = inner_rows(left[...], right[:, columns])
        out_ref[i * width : (i + 1) * width, :] = product.astype(out_ref.dtype)


def pack(keep_ref, other_ref, back_ref, out_ref):
    chips, _, half = keep_ref.shape
    tile = back_ref.shape[2]
    out_ref[:, :, :, :half] = back_ref[...]
    for i in range(3):
        rows = slice(i * tile, (i + 1) * tile)
        total = keep_ref[:, rows, :] + other_ref[:, rows, :].astype(F32)
        if i != 1:
            out_ref[:, i // 2, :, half : 2 * half] = total.astype(BF16)
            continue
        flat = total.reshape(chips * tile, half)
        left, right = flat[:, :LANES], flat[:, LANES:]
        upper = lax.rem(lax.broadcasted_iota(jnp.int32, left.shape, 0), tile) < tile // 2
        first = jnp.where(upper, left, pltpu.roll(right, tile // 2, 0))
        second = jnp.where(upper, pltpu.roll(left, chips * tile - tile // 2, 0), right)
        out_ref[:, 0, :, 2 * half :] = first.astype(BF16).reshape(chips, tile, LANES)
        out_ref[:, 1, :, 2 * half :] = second.astype(BF16).reshape(chips, tile, LANES)


def add_chips(arrived_ref, out_ref):
    chips = arrived_ref.shape[0]
    skip = arrived_ref.shape[3] - out_ref.shape[2]
    total = arrived_ref[0, :, :, skip:].astype(F32)
    for i in range(1, chips):
        total = total + arrived_ref[i, :, :, skip:].astype(F32)
    out_ref[...] = total


def add_pair(own_ref, other_ref, out_ref):
    out_ref[...] = own_ref[...] + other_ref[...]


def add_samples(sibling_ref, own_ref, other_ref, out_ref):
    total = own_ref[...] + other_ref[...]
    tile = total.shape[1]
    half = out_ref.shape[1] // 2
    extra = tile // 2
    whole = jnp.concatenate([total[h, :, :half] for h in range(2)], axis=1)
    parts = [total[h, k * extra : (k + 1) * extra, half:] for h in range(2) for k in range(2)]
    middle = jnp.concatenate(parts, axis=1)

    @pl.when(sibling_ref[0] == 1)
    def _():
        out_ref[:tile, :] = whole
        out_ref[tile:, :] = middle

    @pl.when(sibling_ref[0] == 0)
    def _():
        out_ref[:extra, :] = middle
        out_ref[extra:, :] = whole


def return_grads(
    back_ref, send_rows_ref, send_grad_ref, recv_grad_ref, a_send_ref, a_recv_ref, cot_ref,
    out_ref, spread,
):
    nodes = recv_grad_ref.shape[0]
    slots, groups = send_rows_ref.shape[1:]
    scatter_blocks(spread, back_ref)
    total = send_grad_ref[slots * groups :, :].astype(F32)
    wanted = send_rows_ref[0]
    for j in range(slots):
        arrived = split_load(spread, j, slots, groups).astype(BF16)
        total = total + dot(select_columns(wanted[j : j + 1], nodes), arrived)
    high = total.astype(BF16)
    rest = total - high.astype(F32)
    low = rest.astype(BF16)
    a_send = a_send_ref[...]
    out_ref[0] = (
        cot_ref[0].astype(F32)
        + times_transposed(recv_grad_ref[...], a_recv_ref[...])
        + (times_transposed(high, a_send) + times_transposed(low, a_send))
    )


def shape(dims, dtype):
    return jax.ShapeDtypeStruct(dims, dtype)


def kernel(body, outs, scratch, flops, first=0, space=None, grant=24):
    def call(*operands):
        specs = [
            pl.BlockSpec(memory_space=space if i < first else pltpu.VMEM)
            for i in range(len(operands))
        ]
        moved = sum(x.size * x.dtype.itemsize for x in operands)
        return pl.pallas_call(
            body,
            out_shape=outs,
            in_specs=specs,
            out_specs=jax.tree.map(lambda _: pl.BlockSpec(memory_space=pltpu.VMEM), outs),
            scratch_shapes=scratch,
            compiler_params=pltpu.CompilerParams(vmem_limit_bytes=grant << 20),
            cost_estimate=pl.CostEstimate(flops=flops, bytes_accessed=moved, transcendentals=0),
        )(*operands)

    return call


def exchange(x, axis):
    return lax.all_to_all(x, axis, split_axis=0, concat_axis=0, tiled=True)


def share(keep, send, back, sibling):
    half = keep.shape[1]
    tile = 8
    chips = lax.axis_size("graph_0") * lax.axis_size("graph_1")
    samples = lax.axis_size("sample")
    lanes = 2 * half + half // 2
    other = lax.ppermute(send, "graph_2", [(0, 1), (1, 0)])
    packed = kernel(pack, shape((chips, 2, tile, lanes), BF16), [], 10**7)(
        keep.reshape(chips, -1, half),
        other.reshape(chips, -1, half),
        back.reshape(chips, 2, tile, half),
    )
    arrived = exchange(packed.reshape(2 * chips, tile, lanes), GRAPH)
    own = kernel(add_chips, shape((2, tile, lanes - half), F32), [], 10**7)(
        arrived.reshape(chips, 2, tile, lanes)
    )
    other = lax.ppermute(own, "sample", [(i, i ^ 1) for i in range(samples)])
    own = kernel(add_pair, shape(own.shape, F32), [], 10**6)(own, other)
    other = lax.ppermute(own, "sample", [(i, samples - 1 - i) for i in range(samples)])
    rows = keep.shape[0] // (2 * chips)
    grad_weights = kernel(add_samples, shape((rows, 2 * half), F32), [], 10**6, 1, pltpu.SMEM)(
        sibling, own, other
    )
    return arrived.reshape(2 * chips * tile, lanes), grad_weights


def on_device(
    grid_in,
    mesh_init,
    g2m_geometry,
    w_embed,
    w_g2m,
    w_geo,
    a_send,
    a_recv,
    b_node,
    cotangent,
    g2m_send_rows,
    g2m_counts,
    g2m_senders,
    g2m_receivers,
    mesh_send_rows,
    mesh_senders,
    mesh_receivers,
):
    groups, slots = g2m_send_rows.shape[1:]
    halo_slots = mesh_send_rows.shape[2]
    features = grid_in.shape[2]
    width = w_g2m.shape[1]
    half = width // 2
    nodes = mesh_init.shape[1]
    table_rows = groups * halo_slots + nodes
    halves = 2 * groups * halo_slots

    sibling = 1 - lax.axis_index("graph_2").astype(jnp.int32)[None]
    sibling, g2m_counts = lax.optimization_barrier((sibling, g2m_counts))
    grid_rows = jnp.transpose(g2m_send_rows, (0, 2, 1))
    mesh_rows = jnp.transpose(mesh_send_rows, (0, 2, 1))
    raw_rows = kernel(
        pick_grid,
        shape((groups * slots, features), BF16),
        [
            pltpu.VMEM(grid_rows.shape, jnp.int32),
            pltpu.VMEM(g2m_counts.shape, jnp.int32),
            pltpu.VMEM(grid_in.shape, BF16),
            pltpu.SemaphoreType.DMA((3,)),
            pltpu.VMEM((features // LANES, groups * slots, LANES), F32),
        ],
        10**8,
        3,
        pltpu.HBM,
        GRANTS[0],
    )(grid_rows, g2m_counts, grid_in)
    pieces = exchange(raw_rows.reshape(groups, slots, features), GRAPH)

    latent, halo = kernel(
        encode,
        (shape((nodes, width), BF16), shape((halves, half), BF16)),
        [pltpu.VMEM((half // LANES, halves, LANES), F32)],
        2 * 10**9,
        grant=GRANTS[1],
    )(
        pieces.reshape(groups * slots, features),
        g2m_senders[None],
        g2m_receivers[None],
        g2m_geometry,
        w_embed,
        w_g2m,
        w_geo,
        mesh_init,
        mesh_rows,
    )
    halo = exchange(halo.reshape(groups, 2 * halo_slots, half), GRAPH)

    mesh_out, back, table, send_grad, recv_grad, aggregate, d_update = kernel(
        functools.partial(process, halo_slots),
        (
            shape((1, nodes, width), BF16),
            shape((halves, half), BF16),
            shape((table_rows, width), BF16),
            shape((table_rows, width), BF16),
            shape((nodes, width), BF16),
            shape((nodes, width), BF16),
            shape((nodes, width), BF16),
        ),
        [pltpu.VMEM((half // LANES, halves, LANES), F32)],
        3 * 10**9,
        grant=GRANTS[2],
    )(
        halo.reshape(halves, half),
        latent,
        mesh_senders[None],
        mesh_receivers[None],
        a_send,
        a_recv,
        b_node,
        cotangent,
    )

    operands = (table, send_grad, latent, recv_grad, aggregate, d_update)
    send = kernel(functools.partial(weight_grads, False), shape((3 * width, half), BF16), [], 5 * 10**8, 1, pltpu.SMEM)(sibling, *operands)
    keep = kernel(functools.partial(weight_grads, True), shape((3 * width, half), F32), [], 5 * 10**8, 1, pltpu.SMEM)(sibling, *operands)
    arrived, grad_weights = share(keep, send, back, sibling)

    grad_mesh = kernel(
        return_grads,
        shape((1, nodes, width), F32),
        [pltpu.VMEM((half // LANES, halves, LANES), F32)],
        10**9,
    )(
        arrived,
        mesh_rows,
        send_grad,
        recv_grad,
        a_send,
        a_recv,
        cotangent,
    )
    return (mesh_out, grad_mesh, grad_weights)


def solution(mesh):
    torus = Mesh(
        mesh.devices.reshape(8, 8, 2, mesh.shape["sample"]),
        ("graph_0", "graph_1", "graph_2", "sample"),
    )
    in_specs = (
        P("sample", GRAPH, None),
        P("sample", GRAPH, None),
        P(None, GRAPH),
        P(),
        P(),
        P(),
        P(),
        P(),
        P(),
        P("sample", GRAPH, None),
        P(GRAPH, None, None),
        P(GRAPH, None),
        P(GRAPH),
        P(GRAPH),
        P(GRAPH, None, None),
        P(GRAPH),
        P(GRAPH),
    )
    out_specs = (P("sample", GRAPH, None), P("sample", GRAPH, None), P(GRAPH, None))
    return jax.shard_map(
        on_device, mesh=torus, in_specs=in_specs, out_specs=out_specs, check_vma=False
    )
```

```python
import functools

import jax
import jax.numpy as jnp
from jax import lax
from jax.experimental import pallas as pl
from jax.experimental.pallas import tpu as pltpu
from jax.sharding import Mesh
from jax.sharding import PartitionSpec as P

GRAPH = ("graph_0", "graph_1", "graph_2")
LANES = 128
F32 = jnp.float32
BF16 = jnp.bfloat16
GRANTS = (60, 40, 40)


def dot(left, right):
    return jnp.dot(left, right, preferred_element_type=F32)


def times_transposed(left, right):
    return lax.dot_general(left, right, (((1,), (1,)), ((), ())), preferred_element_type=F32)


def inner_rows(left, right):
    return lax.dot_general(left, right, (((0,), (0,)), ((), ())), preferred_element_type=F32)


def logistic(v):
    return 0.5 * jnp.tanh(0.5 * v) + 0.5


def silu(v):
    return v * logistic(v)


def slope_from(v, s):
    return s * (1.0 + v * (1.0 - s))


def columns_of(row):
    return jnp.transpose(jnp.broadcast_to(row, (LANES, row.shape[1])))


def slot_columns(ids):
    slots, groups = ids.shape
    turned = jnp.transpose(jnp.concatenate([ids] * (LANES // slots), axis=0))
    return [jnp.broadcast_to(turned[:, j : j + 1], (groups, LANES)) for j in range(slots)]


def select_rows(column, size):
    lane = lax.broadcasted_iota(jnp.int32, column.shape, 1)
    blocks = [
        jnp.where(column == lane + LANES * k, 1.0, 0.0).astype(BF16) for k in range(size // LANES)
    ]
    return blocks[0] if len(blocks) == 1 else jnp.concatenate(blocks, axis=1)


def select_columns(row, size):
    segment = lax.broadcasted_iota(jnp.int32, (size, row.shape[1]), 0)
    return jnp.where(segment == row, 1.0, 0.0).astype(BF16)


def strided_store(spread, start, stride, value):
    rows, width = value.shape
    for k in range(width // LANES):
        spread[k, pl.ds(start, rows, stride=stride), :] = value[:, k * LANES : (k + 1) * LANES]


def gather_blocks(spread, out_ref):
    for k in range(spread.shape[0]):
        out_ref[:, k * LANES : (k + 1) * LANES] = spread[k].astype(out_ref.dtype)


def scatter_blocks(spread, in_ref):
    for k in range(spread.shape[0]):
        spread[k] = in_ref[:, k * LANES : (k + 1) * LANES].astype(spread.dtype)


def pick_grid(rows_hbm, counts_hbm, grid_hbm, out_ref, rows, counts, grid, sems, spread):
    copies = [
        pltpu.make_async_copy(source, target, sems.at[i])
        for i, (source, target) in enumerate(
            ((rows_hbm, rows), (counts_hbm, counts), (grid_hbm, grid))
        )
    ]
    for copy in copies:
        copy.start()
    copies[0].wait()
    copies[1].wait()
    slots = rows.shape[1]
    slot = lax.broadcasted_iota(jnp.int32, rows.shape[1:], 0)
    ids = slot_columns(jnp.where(slot < counts[...], rows[0], -1))
    chosen = jnp.concatenate([select_rows(column, grid.shape[1]) for column in ids], axis=0)
    copies[2].wait()
    picked = dot(chosen, grid[0])
    groups = rows.shape[2]
    for j in range(slots):
        strided_store(spread, j, slots, picked[j * groups : (j + 1) * groups])
    gather_blocks(spread, out_ref)


def encode(
    pieces_ref, senders_ref, receivers_ref, geometry_ref, w_embed_ref, w_g2m_ref, w_geo_ref,
    init_ref, send_rows_ref, latent_ref, halo_ref, spread,
):
    edges = senders_ref.shape[1]
    nodes, width = latent_ref.shape
    inputs = geometry_ref.shape[0]
    geometry = geometry_ref[...].astype(F32)
    blank = jnp.zeros((LANES - inputs, edges), F32)
    geometry = jnp.transpose(jnp.concatenate([geometry, blank], axis=0)).astype(BF16)
    blank = jnp.zeros((LANES - inputs, width), F32)
    weights = [w_g2m_ref[...].astype(F32), w_geo_ref[...].astype(F32), blank]
    weights = jnp.concatenate(weights, axis=0).astype(BF16)
    chosen = select_rows(columns_of(senders_ref[...]), pieces_ref.shape[0])
    raw = dot(chosen, pieces_ref[...]).astype(BF16)
    embedded = silu(dot(raw, w_embed_ref[...])).astype(BF16)
    message = silu(dot(jnp.concatenate([embedded, geometry], axis=1), weights)).astype(BF16)
    gather = select_columns(receivers_ref[...], nodes)
    total = init_ref[0].astype(F32) + dot(gather, message)
    latent = total.astype(BF16)
    latent_ref[...] = latent
    ids = slot_columns(send_rows_ref[0])
    picked = dot(jnp.concatenate([select_rows(column, nodes) for column in ids], axis=0), latent)
    groups = send_rows_ref.shape[2]
    for j in range(len(ids)):
        split_store(spread, j, len(ids), picked[j * groups : (j + 1) * groups])
    gather_blocks(spread, halo_ref)


def split_store(spread, j, slots, value):
    groups, width = value.shape
    strided_store(spread, j, 2 * slots, value[:, : width // 2])
    strided_store(spread, slots + j, 2 * slots, value[:, width // 2 :])


def split_load(spread, j, slots, groups):
    blocks = [
        spread[k, pl.ds(start, groups, stride=2 * slots), :]
        for start in (j, slots + j)
        for k in range(spread.shape[0])
    ]
    return jnp.concatenate(blocks, axis=1)


def weight_grads(
    mine, sibling_ref, table_ref, send_grad_ref, latent_ref, recv_grad_ref, aggregate_ref,
    d_update_ref, out_ref,
):
    half = out_ref.shape[1]
    width = latent_ref.shape[1]
    core = 1 - sibling_ref[0] if mine else sibling_ref[0]
    columns = pl.ds(pl.multiple_of(core * half, half), half)
    pairs = ((table_ref, send_grad_ref), (latent_ref, recv_grad_ref), (aggregate_ref, d_update_ref))
    for i, (left, right) in enumerate(pairs):
        product = inner_rows(left[...], right[:, columns])
        out_ref[i * width : (i + 1) * width, :] = product.astype(out_ref.dtype)


def process(
    slots, sibling_ref, halo_ref, latent_ref, senders_ref, receivers_ref, a_send_ref, a_recv_ref, b_node_ref,
    cot_ref,
    out_ref, back_ref, table_ref, send_grad_ref, recv_grad_ref, aggregate_ref, d_update_ref, send_ref,
    spread,
):
    nodes, width = latent_ref.shape
    rows = table_ref.shape[0]
    remote = rows - nodes
    groups = remote // slots
    scatter_blocks(spread, halo_ref)
    for j in range(slots):
        table_ref[j * groups : (j + 1) * groups, :] = split_load(spread, j, slots, groups).astype(BF16)
    latent = latent_ref[...]
    table_ref[remote:, :] = latent
    ids = senders_ref[...]
    ids = jnp.where(ids < remote, lax.rem(ids, slots) * groups + lax.div(ids, slots), ids)
    receivers = receivers_ref[...]
    receive = select_rows(columns_of(receivers), nodes)
    gather = select_columns(receivers, nodes)
    sent = dot(select_rows(columns_of(ids), rows), table_ref[...]).astype(BF16)
    own = dot(receive, latent).astype(BF16)
    weights = jnp.concatenate([a_send_ref[...], a_recv_ref[...]], axis=0)
    pre_act = dot(jnp.concatenate([sent, own], axis=1), weights)
    gate = logistic(pre_act)
    aggregate = dot(gather, (pre_act * gate).astype(BF16)).astype(BF16)
    aggregate_ref[...] = aggregate
    update = dot(aggregate, b_node_ref[...])
    update_gate = logistic(update)
    out_ref[0] = (latent.astype(F32) + update * update_gate).astype(BF16)
    d_update = (cot_ref[0].astype(F32) * slope_from(update, update_gate)).astype(BF16)
    d_update_ref[...] = d_update
    d_aggregate = times_transposed(d_update, b_node_ref[...]).astype(BF16)
    d_pre = (dot(receive, d_aggregate) * slope_from(pre_act, gate)).astype(BF16)
    sums = dot(jnp.concatenate([select_columns(ids, rows), gather], axis=0), d_pre)
    recv_grad_ref[...] = sums[rows:].astype(BF16)
    send_grad = sums[:rows]
    send_grad_ref[...] = send_grad.astype(BF16)
    for j in range(slots):
        split_store(spread, j, slots, send_grad[j * groups : (j + 1) * groups])
    gather_blocks(spread, back_ref)
    weight_grads(
        False, sibling_ref, table_ref, send_grad_ref, latent_ref, recv_grad_ref, aggregate_ref,
        d_update_ref, send_ref,
    )


def pack(keep_ref, other_ref, back_ref, out_ref):
    chips, _, half = keep_ref.shape
    tile = back_ref.shape[2]
    out_ref[:, :, :, :half] = back_ref[...]
    for i in range(3):
        rows = slice(i * tile, (i + 1) * tile)
        total = keep_ref[:, rows, :] + other_ref[:, rows, :].astype(F32)
        if i != 1:
            out_ref[:, i // 2, :, half : 2 * half] = total.astype(BF16)
            continue
        flat = total.reshape(chips * tile, half)
        left, right = flat[:, :LANES], flat[:, LANES:]
        upper = lax.rem(lax.broadcasted_iota(jnp.int32, left.shape, 0), tile) < tile // 2
        first = jnp.where(upper, left, pltpu.roll(right, tile // 2, 0))
        second = jnp.where(upper, pltpu.roll(left, chips * tile - tile // 2, 0), right)
        out_ref[:, 0, :, 2 * half :] = first.astype(BF16).reshape(chips, tile, LANES)
        out_ref[:, 1, :, 2 * half :] = second.astype(BF16).reshape(chips, tile, LANES)


def add_chips(arrived_ref, out_ref):
    chips = arrived_ref.shape[0]
    skip = arrived_ref.shape[3] - out_ref.shape[3]
    total = arrived_ref[0, :, :, skip:].astype(F32)
    for i in range(1, chips):
        total = total + arrived_ref[i, :, :, skip:].astype(F32)
    for i in range(out_ref.shape[0]):
        out_ref[i] = total


def add_samples(sibling_ref, arrived_ref, out_ref):
    total = arrived_ref[0]
    for i in range(1, arrived_ref.shape[0]):
        total = total + arrived_ref[i]
    tile = total.shape[1]
    half = out_ref.shape[1] // 2
    extra = tile // 2
    whole = jnp.concatenate([total[h, :, :half] for h in range(2)], axis=1)
    parts = [total[h, k * extra : (k + 1) * extra, half:] for h in range(2) for k in range(2)]
    middle = jnp.concatenate(parts, axis=1)

    @pl.when(sibling_ref[0] == 1)
    def _():
        out_ref[:tile, :] = whole
        out_ref[tile:, :] = middle

    @pl.when(sibling_ref[0] == 0)
    def _():
        out_ref[:extra, :] = middle
        out_ref[extra:, :] = whole


def return_grads(
    back_ref, send_rows_ref, send_grad_ref, recv_grad_ref, a_send_ref, a_recv_ref, cot_ref,
    out_ref, spread,
):
    nodes = recv_grad_ref.shape[0]
    slots, groups = send_rows_ref.shape[1:]
    scatter_blocks(spread, back_ref)
    wanted = send_rows_ref[0]
    arrived = [split_load(spread, j, slots, groups).astype(BF16) for j in range(slots)]
    chosen = [select_columns(wanted[j : j + 1], nodes) for j in range(slots)]
    total = dot(jnp.concatenate(chosen, axis=1), jnp.concatenate(arrived, axis=0))
    total = total + send_grad_ref[slots * groups :, :].astype(F32)
    high = total.astype(BF16)
    rest = total - high.astype(F32)
    low = rest.astype(BF16)
    a_send = a_send_ref[...]
    out_ref[0] = (
        cot_ref[0].astype(F32)
        + times_transposed(recv_grad_ref[...], a_recv_ref[...])
        + (times_transposed(high, a_send) + times_transposed(low, a_send))
    )


def shape(dims, dtype):
    return jax.ShapeDtypeStruct(dims, dtype)


def kernel(body, outs, scratch, flops, first=0, space=None, grant=24):
    def call(*operands):
        specs = [
            pl.BlockSpec(memory_space=space if i < first else pltpu.VMEM)
            for i in range(len(operands))
        ]
        moved = sum(x.size * x.dtype.itemsize for x in operands)
        return pl.pallas_call(
            body,
            out_shape=outs,
            in_specs=specs,
            out_specs=jax.tree.map(lambda _: pl.BlockSpec(memory_space=pltpu.VMEM), outs),
            scratch_shapes=scratch,
            compiler_params=pltpu.CompilerParams(vmem_limit_bytes=grant << 20),
            cost_estimate=pl.CostEstimate(flops=flops, bytes_accessed=moved, transcendentals=0),
        )(*operands)

    return call


def exchange(x, axis):
    return lax.all_to_all(x, axis, split_axis=0, concat_axis=0, tiled=True)


def share(keep, send, back, sibling):
    half = keep.shape[1]
    tile = 8
    chips = lax.axis_size("graph_0") * lax.axis_size("graph_1")
    samples = lax.axis_size("sample")
    lanes = 2 * half + half // 2
    other = lax.ppermute(send, "graph_2", [(0, 1), (1, 0)])
    packed = kernel(pack, shape((chips, 2, tile, lanes), BF16), [], 10**7)(
        keep.reshape(chips, -1, half),
        other.reshape(chips, -1, half),
        back.reshape(chips, 2, tile, half),
    )
    arrived = exchange(packed.reshape(2 * chips, tile, lanes), GRAPH)
    copies = kernel(add_chips, shape((samples, 2, tile, lanes - half), F32), [], 10**7)(
        arrived.reshape(chips, 2, tile, lanes)
    )
    copies = exchange(copies, "sample")
    rows = keep.shape[0] // (2 * chips)
    grad_weights = kernel(add_samples, shape((rows, 2 * half), F32), [], 10**6, 1, pltpu.SMEM)(
        sibling, copies
    )
    return arrived.reshape(2 * chips * tile, lanes), grad_weights


def on_device(
    grid_in,
    mesh_init,
    g2m_geometry,
    w_embed,
    w_g2m,
    w_geo,
    a_send,
    a_recv,
    b_node,
    cotangent,
    g2m_send_rows,
    g2m_counts,
    g2m_senders,
    g2m_receivers,
    mesh_send_rows,
    mesh_senders,
    mesh_receivers,
):
    groups, slots = g2m_send_rows.shape[1:]
    halo_slots = mesh_send_rows.shape[2]
    features = grid_in.shape[2]
    width = w_g2m.shape[1]
    half = width // 2
    nodes = mesh_init.shape[1]
    table_rows = groups * halo_slots + nodes
    halves = 2 * groups * halo_slots

    sibling = 1 - lax.axis_index("graph_2").astype(jnp.int32)[None]
    sibling, g2m_counts = lax.optimization_barrier((sibling, g2m_counts))
    grid_rows = jnp.transpose(g2m_send_rows, (0, 2, 1))
    mesh_rows = jnp.transpose(mesh_send_rows, (0, 2, 1))
    raw_rows = kernel(
        pick_grid,
        shape((groups * slots, features), BF16),
        [
            pltpu.VMEM(grid_rows.shape, jnp.int32),
            pltpu.VMEM(g2m_counts.shape, jnp.int32),
            pltpu.VMEM(grid_in.shape, BF16),
            pltpu.SemaphoreType.DMA((3,)),
            pltpu.VMEM((features // LANES, groups * slots, LANES), F32),
        ],
        10**8,
        3,
        pltpu.HBM,
        GRANTS[0],
    )(grid_rows, g2m_counts, grid_in)
    pieces = exchange(raw_rows.reshape(groups, slots, features), GRAPH)

    latent, halo = kernel(
        encode,
        (shape((nodes, width), BF16), shape((halves, half), BF16)),
        [pltpu.VMEM((half // LANES, halves, LANES), F32)],
        2 * 10**9,
        grant=GRANTS[1],
    )(
        pieces.reshape(groups * slots, features),
        g2m_senders[None],
        g2m_receivers[None],
        g2m_geometry,
        w_embed,
        w_g2m,
        w_geo,
        mesh_init,
        mesh_rows,
    )
    halo = exchange(halo.reshape(groups, 2 * halo_slots, half), GRAPH)

    mesh_out, back, table, send_grad, recv_grad, aggregate, d_update, send = kernel(
        functools.partial(process, halo_slots),
        (
            shape((1, nodes, width), BF16),
            shape((halves, half), BF16),
            shape((table_rows, width), BF16),
            shape((table_rows, width), BF16),
            shape((nodes, width), BF16),
            shape((nodes, width), BF16),
            shape((nodes, width), BF16),
            shape((3 * width, half), BF16),
        ),
        [pltpu.VMEM((half // LANES, halves, LANES), F32)],
        3 * 10**9,
        1,
        pltpu.SMEM,
        GRANTS[2],
    )(
        sibling,
        halo.reshape(halves, half),
        latent,
        mesh_senders[None],
        mesh_receivers[None],
        a_send,
        a_recv,
        b_node,
        cotangent,
    )

    operands = (table, send_grad, latent, recv_grad, aggregate, d_update)
    keep = kernel(functools.partial(weight_grads, True), shape((3 * width, half), F32), [], 5 * 10**8, 1, pltpu.SMEM)(sibling, *operands)
    arrived, grad_weights = share(keep, send, back, sibling)

    grad_mesh = kernel(
        return_grads,
        shape((1, nodes, width), F32),
        [pltpu.VMEM((half // LANES, halves, LANES), F32)],
        10**9,
    )(
        arrived,
        mesh_rows,
        send_grad,
        recv_grad,
        a_send,
        a_recv,
        cotangent,
    )
    return (mesh_out, grad_mesh, grad_weights)


def solution(mesh):
    torus = Mesh(
        mesh.devices.reshape(8, 8, 2, mesh.shape["sample"]),
        ("graph_0", "graph_1", "graph_2", "sample"),
    )
    in_specs = (
        P("sample", GRAPH, None),
        P("sample", GRAPH, None),
        P(None, GRAPH),
        P(),
        P(),
        P(),
        P(),
        P(),
        P(),
        P("sample", GRAPH, None),
        P(GRAPH, None, None),
        P(GRAPH, None),
        P(GRAPH),
        P(GRAPH),
        P(GRAPH, None, None),
        P(GRAPH),
        P(GRAPH),
    )
    out_specs = (P("sample", GRAPH, None), P("sample", GRAPH, None), P(GRAPH, None))
    return jax.shard_map(
        on_device, mesh=torus, in_specs=in_specs, out_specs=out_specs, check_vma=False
    )
```

```python
import functools

import jax
import jax.numpy as jnp
from jax import lax
from jax.experimental import pallas as pl
from jax.experimental.pallas import tpu as pltpu
from jax.sharding import Mesh
from jax.sharding import PartitionSpec as P

GRAPH = ("graph_0", "graph_1", "graph_2")
LANES = 128
F32 = jnp.float32
BF16 = jnp.bfloat16
GRANTS = (60, 40, 40)


def dot(left, right):
    return jnp.dot(left, right, preferred_element_type=F32)


def times_transposed(left, right):
    return lax.dot_general(left, right, (((1,), (1,)), ((), ())), preferred_element_type=F32)


def inner_rows(left, right):
    return lax.dot_general(left, right, (((0,), (0,)), ((), ())), preferred_element_type=F32)


def logistic(v):
    return 1.0 / (1.0 + jnp.exp(-v))


def silu(v):
    return v * logistic(v)


def slope_from(v, s):
    return s * (1.0 + v * (1.0 - s))


def columns_of(row):
    return jnp.transpose(jnp.broadcast_to(row, (LANES, row.shape[1])))


def slot_columns(ids):
    slots, groups = ids.shape
    turned = jnp.transpose(jnp.concatenate([ids] * (LANES // slots), axis=0))
    return [jnp.broadcast_to(turned[:, j : j + 1], (groups, LANES)) for j in range(slots)]


def select_rows(column, size):
    lane = lax.broadcasted_iota(jnp.int32, column.shape, 1)
    blocks = [
        jnp.where(column == lane + LANES * k, 1.0, 0.0).astype(BF16) for k in range(size // LANES)
    ]
    return blocks[0] if len(blocks) == 1 else jnp.concatenate(blocks, axis=1)


def select_columns(row, size):
    segment = lax.broadcasted_iota(jnp.int32, (size, row.shape[1]), 0)
    return jnp.where(segment == row, 1.0, 0.0).astype(BF16)


def strided_store(spread, start, stride, value):
    rows, width = value.shape
    for k in range(width // LANES):
        spread[k, pl.ds(start, rows, stride=stride), :] = value[:, k * LANES : (k + 1) * LANES]


def gather_blocks(spread, out_ref):
    for k in range(spread.shape[0]):
        out_ref[:, k * LANES : (k + 1) * LANES] = spread[k].astype(out_ref.dtype)


def scatter_blocks(spread, in_ref):
    for k in range(spread.shape[0]):
        spread[k] = in_ref[:, k * LANES : (k + 1) * LANES].astype(spread.dtype)


def pick_grid(rows_hbm, counts_hbm, grid_hbm, out_ref, rows, counts, grid, sems, spread):
    copies = [
        pltpu.make_async_copy(source, target, sems.at[i])
        for i, (source, target) in enumerate(
            ((rows_hbm, rows), (counts_hbm, counts), (grid_hbm, grid))
        )
    ]
    for copy in copies:
        copy.start()
    copies[0].wait()
    copies[1].wait()
    slots = rows.shape[1]
    slot = lax.broadcasted_iota(jnp.int32, rows.shape[1:], 0)
    ids = slot_columns(jnp.where(slot < counts[...], rows[0], -1))
    chosen = jnp.concatenate([select_rows(column, grid.shape[1]) for column in ids], axis=0)
    copies[2].wait()
    picked = dot(chosen, grid[0])
    groups = rows.shape[2]
    for j in range(slots):
        strided_store(spread, j, slots, picked[j * groups : (j + 1) * groups])
    gather_blocks(spread, out_ref)


def encode(
    pieces_ref, senders_ref, receivers_ref, geometry_ref, w_embed_ref, w_g2m_ref, w_geo_ref,
    init_ref, send_rows_ref, latent_ref, halo_ref, spread,
):
    edges = senders_ref.shape[1]
    nodes, width = latent_ref.shape
    inputs = geometry_ref.shape[0]
    geometry = geometry_ref[...].astype(F32)
    blank = jnp.zeros((LANES - inputs, edges), F32)
    geometry = jnp.transpose(jnp.concatenate([geometry, blank], axis=0)).astype(BF16)
    blank = jnp.zeros((LANES - inputs, width), F32)
    weights = [w_g2m_ref[...].astype(F32), w_geo_ref[...].astype(F32), blank]
    weights = jnp.concatenate(weights, axis=0).astype(BF16)
    chosen = select_rows(columns_of(senders_ref[...]), pieces_ref.shape[0])
    raw = dot(chosen, pieces_ref[...]).astype(BF16)
    embedded = silu(dot(raw, w_embed_ref[...])).astype(BF16)
    message = silu(dot(jnp.concatenate([embedded, geometry], axis=1), weights)).astype(BF16)
    gather = select_columns(receivers_ref[...], nodes)
    total = init_ref[0].astype(F32) + dot(gather, message)
    latent = total.astype(BF16)
    latent_ref[...] = latent
    ids = slot_columns(send_rows_ref[0])
    picked = dot(jnp.concatenate([select_rows(column, nodes) for column in ids], axis=0), latent)
    groups = send_rows_ref.shape[2]
    for j in range(len(ids)):
        split_store(spread, j, len(ids), picked[j * groups : (j + 1) * groups])
    gather_blocks(spread, halo_ref)


def split_store(spread, j, slots, value):
    groups, width = value.shape
    strided_store(spread, j, 2 * slots, value[:, : width // 2])
    strided_store(spread, slots + j, 2 * slots, value[:, width // 2 :])


def split_load(spread, j, slots, groups):
    blocks = [
        spread[k, pl.ds(start, groups, stride=2 * slots), :]
        for start in (j, slots + j)
        for k in range(spread.shape[0])
    ]
    return jnp.concatenate(blocks, axis=1)


def weight_grads(
    mine, sibling_ref, table_ref, send_grad_ref, latent_ref, recv_grad_ref, aggregate_ref,
    d_update_ref, out_ref,
):
    half = out_ref.shape[1]
    width = latent_ref.shape[1]
    core = 1 - sibling_ref[0] if mine else sibling_ref[0]
    columns = pl.ds(pl.multiple_of(core * half, half), half)
    pairs = ((table_ref, send_grad_ref), (latent_ref, recv_grad_ref), (aggregate_ref, d_update_ref))
    for i, (left, right) in enumerate(pairs):
        product = inner_rows(left[...], right[:, columns])
        out_ref[i * width : (i + 1) * width, :] = product.astype(out_ref.dtype)


def process(
    slots, sibling_ref, halo_ref, latent_ref, senders_ref, receivers_ref, a_send_ref, a_recv_ref, b_node_ref,
    cot_ref,
    out_ref, back_ref, table_ref, send_grad_ref, recv_grad_ref, aggregate_ref, d_update_ref, send_ref,
    spread,
):
    nodes, width = latent_ref.shape
    rows = table_ref.shape[0]
    remote = rows - nodes
    groups = remote // slots
    scatter_blocks(spread, halo_ref)
    for j in range(slots):
        table_ref[j * groups : (j + 1) * groups, :] = split_load(spread, j, slots, groups).astype(BF16)
    latent = latent_ref[...]
    table_ref[remote:, :] = latent
    ids = senders_ref[...]
    ids = jnp.where(ids < remote, lax.rem(ids, slots) * groups + lax.div(ids, slots), ids)
    receivers = receivers_ref[...]
    receive = select_rows(columns_of(receivers), nodes)
    gather = select_columns(receivers, nodes)
    sent = dot(select_rows(columns_of(ids), rows), table_ref[...]).astype(BF16)
    own = dot(receive, latent).astype(BF16)
    weights = jnp.concatenate([a_send_ref[...], a_recv_ref[...]], axis=0)
    pre_act = dot(jnp.concatenate([sent, own], axis=1), weights)
    gate = logistic(pre_act)
    aggregate = dot(gather, (pre_act * gate).astype(BF16)).astype(BF16)
    aggregate_ref[...] = aggregate
    update = dot(aggregate, b_node_ref[...])
    update_gate = logistic(update)
    out_ref[0] = (latent.astype(F32) + update * update_gate).astype(BF16)
    d_update = (cot_ref[0].astype(F32) * slope_from(update, update_gate)).astype(BF16)
    d_update_ref[...] = d_update
    d_aggregate = times_transposed(d_update, b_node_ref[...]).astype(BF16)
    d_pre = (dot(receive, d_aggregate) * slope_from(pre_act, gate)).astype(BF16)
    sums = dot(jnp.concatenate([select_columns(ids, rows), gather], axis=0), d_pre)
    recv_grad_ref[...] = sums[rows:].astype(BF16)
    send_grad = sums[:rows]
    send_grad_ref[...] = send_grad.astype(BF16)
    for j in range(slots):
        split_store(spread, j, slots, send_grad[j * groups : (j + 1) * groups])
    gather_blocks(spread, back_ref)
    weight_grads(
        False, sibling_ref, table_ref, send_grad_ref, latent_ref, recv_grad_ref, aggregate_ref,
        d_update_ref, send_ref,
    )


def pack(keep_ref, other_ref, back_ref, out_ref):
    chips, _, half = keep_ref.shape
    tile = back_ref.shape[2]
    out_ref[:, :, :, :half] = back_ref[...]
    for i in range(3):
        rows = slice(i * tile, (i + 1) * tile)
        total = keep_ref[:, rows, :] + other_ref[:, rows, :].astype(F32)
        if i != 1:
            out_ref[:, i // 2, :, half : 2 * half] = total.astype(BF16)
            continue
        flat = total.reshape(chips * tile, half)
        left, right = flat[:, :LANES], flat[:, LANES:]
        upper = lax.rem(lax.broadcasted_iota(jnp.int32, left.shape, 0), tile) < tile // 2
        first = jnp.where(upper, left, pltpu.roll(right, tile // 2, 0))
        second = jnp.where(upper, pltpu.roll(left, chips * tile - tile // 2, 0), right)
        out_ref[:, 0, :, 2 * half :] = first.astype(BF16).reshape(chips, tile, LANES)
        out_ref[:, 1, :, 2 * half :] = second.astype(BF16).reshape(chips, tile, LANES)


def add_chips(arrived_ref, out_ref):
    chips = arrived_ref.shape[0]
    skip = arrived_ref.shape[3] - out_ref.shape[3]
    total = arrived_ref[0, :, :, skip:].astype(F32)
    for i in range(1, chips):
        total = total + arrived_ref[i, :, :, skip:].astype(F32)
    for i in range(out_ref.shape[0]):
        out_ref[i] = total


def add_samples(sibling_ref, arrived_ref, out_ref):
    total = arrived_ref[0]
    for i in range(1, arrived_ref.shape[0]):
        total = total + arrived_ref[i]
    tile = total.shape[1]
    half = out_ref.shape[1] // 2
    extra = tile // 2
    whole = jnp.concatenate([total[h, :, :half] for h in range(2)], axis=1)
    parts = [total[h, k * extra : (k + 1) * extra, half:] for h in range(2) for k in range(2)]
    middle = jnp.concatenate(parts, axis=1)

    @pl.when(sibling_ref[0] == 1)
    def _():
        out_ref[:tile, :] = whole
        out_ref[tile:, :] = middle

    @pl.when(sibling_ref[0] == 0)
    def _():
        out_ref[:extra, :] = middle
        out_ref[extra:, :] = whole


def return_grads(
    back_ref, send_rows_ref, send_grad_ref, recv_grad_ref, a_send_ref, a_recv_ref, cot_ref,
    out_ref, spread,
):
    nodes = recv_grad_ref.shape[0]
    slots, groups = send_rows_ref.shape[1:]
    scatter_blocks(spread, back_ref)
    wanted = send_rows_ref[0]
    arrived = [split_load(spread, j, slots, groups).astype(BF16) for j in range(slots)]
    chosen = [select_columns(wanted[j : j + 1], nodes) for j in range(slots)]
    total = dot(jnp.concatenate(chosen, axis=1), jnp.concatenate(arrived, axis=0))
    total = total + send_grad_ref[slots * groups :, :].astype(F32)
    high = total.astype(BF16)
    rest = total - high.astype(F32)
    low = rest.astype(BF16)
    a_send = a_send_ref[...]
    out_ref[0] = (
        cot_ref[0].astype(F32)
        + times_transposed(recv_grad_ref[...], a_recv_ref[...])
        + (times_transposed(high, a_send) + times_transposed(low, a_send))
    )


def shape(dims, dtype):
    return jax.ShapeDtypeStruct(dims, dtype)


def kernel(body, outs, scratch, flops, first=0, space=None, grant=24):
    def call(*operands):
        specs = [
            pl.BlockSpec(memory_space=space if i < first else pltpu.VMEM)
            for i in range(len(operands))
        ]
        moved = sum(x.size * x.dtype.itemsize for x in operands)
        return pl.pallas_call(
            body,
            out_shape=outs,
            in_specs=specs,
            out_specs=jax.tree.map(lambda _: pl.BlockSpec(memory_space=pltpu.VMEM), outs),
            scratch_shapes=scratch,
            compiler_params=pltpu.CompilerParams(vmem_limit_bytes=grant << 20),
            cost_estimate=pl.CostEstimate(flops=flops, bytes_accessed=moved, transcendentals=0),
        )(*operands)

    return call


def exchange(x, axis):
    return lax.all_to_all(x, axis, split_axis=0, concat_axis=0, tiled=True)


def share(keep, send, back, core):
    half = keep.shape[1]
    tile = 8
    chips = lax.axis_size("graph_0") * lax.axis_size("graph_1")
    samples = lax.axis_size("sample")
    lanes = 2 * half + half // 2
    other = lax.ppermute(send, "graph_2", [(0, 1), (1, 0)])
    packed = kernel(pack, shape((chips, 2, tile, lanes), BF16), [], 10**7)(
        keep.reshape(chips, -1, half),
        other.reshape(chips, -1, half),
        back.reshape(chips, 2, tile, half),
    )
    arrived = exchange(packed.reshape(2 * chips, tile, lanes), GRAPH)
    arrived, core = lax.optimization_barrier((arrived, core))
    copies = kernel(add_chips, shape((samples, 2, tile, lanes - half), F32), [], 10**7)(
        arrived.reshape(chips, 2, tile, lanes)
    )
    copies = exchange(copies, "sample")
    rows = keep.shape[0] // (2 * chips)
    grad_weights = kernel(add_samples, shape((rows, 2 * half), F32), [], 10**6, 1, pltpu.SMEM)(
        1 - core, copies
    )
    return arrived.reshape(2 * chips * tile, lanes), grad_weights


def on_device(
    grid_in,
    mesh_init,
    g2m_geometry,
    w_embed,
    w_g2m,
    w_geo,
    a_send,
    a_recv,
    b_node,
    cotangent,
    g2m_send_rows,
    g2m_counts,
    g2m_senders,
    g2m_receivers,
    mesh_send_rows,
    mesh_senders,
    mesh_receivers,
):
    groups, slots = g2m_send_rows.shape[1:]
    halo_slots = mesh_send_rows.shape[2]
    features = grid_in.shape[2]
    width = w_g2m.shape[1]
    half = width // 2
    nodes = mesh_init.shape[1]
    table_rows = groups * halo_slots + nodes
    halves = 2 * groups * halo_slots

    core = lax.axis_index("graph_2").astype(jnp.int32)[None]
    core, g2m_counts = lax.optimization_barrier((core, g2m_counts))
    grid_rows = jnp.transpose(g2m_send_rows, (0, 2, 1))
    mesh_rows = jnp.transpose(mesh_send_rows, (0, 2, 1))
    raw_rows = kernel(
        pick_grid,
        shape((groups * slots, features), BF16),
        [
            pltpu.VMEM(grid_rows.shape, jnp.int32),
            pltpu.VMEM(g2m_counts.shape, jnp.int32),
            pltpu.VMEM(grid_in.shape, BF16),
            pltpu.SemaphoreType.DMA((3,)),
            pltpu.VMEM((features // LANES, groups * slots, LANES), F32),
        ],
        10**8,
        3,
        pltpu.HBM,
        GRANTS[0],
    )(grid_rows, g2m_counts, grid_in)
    pieces = exchange(raw_rows.reshape(groups, slots, features), GRAPH)

    latent, halo = kernel(
        encode,
        (shape((nodes, width), BF16), shape((halves, half), BF16)),
        [pltpu.VMEM((half // LANES, halves, LANES), F32)],
        2 * 10**9,
        grant=GRANTS[1],
    )(
        pieces.reshape(groups * slots, features),
        g2m_senders[None],
        g2m_receivers[None],
        g2m_geometry,
        w_embed,
        w_g2m,
        w_geo,
        mesh_init,
        mesh_rows,
    )
    halo = exchange(halo.reshape(groups, 2 * halo_slots, half), GRAPH)
    halo, core = lax.optimization_barrier((halo, core))
    sibling = 1 - core

    mesh_out, back, table, send_grad, recv_grad, aggregate, d_update, send = kernel(
        functools.partial(process, halo_slots),
        (
            shape((1, nodes, width), BF16),
            shape((halves, half), BF16),
            shape((table_rows, width), BF16),
            shape((table_rows, width), BF16),
            shape((nodes, width), BF16),
            shape((nodes, width), BF16),
            shape((nodes, width), BF16),
            shape((3 * width, half), BF16),
        ),
        [pltpu.VMEM((half // LANES, halves, LANES), F32)],
        3 * 10**9,
        1,
        pltpu.SMEM,
        GRANTS[2],
    )(
        sibling,
        halo.reshape(halves, half),
        latent,
        mesh_senders[None],
        mesh_receivers[None],
        a_send,
        a_recv,
        b_node,
        cotangent,
    )

    operands = (table, send_grad, latent, recv_grad, aggregate, d_update)
    keep = kernel(functools.partial(weight_grads, True), shape((3 * width, half), F32), [], 5 * 10**8, 1, pltpu.SMEM)(sibling, *operands)
    arrived, grad_weights = share(keep, send, back, core)

    grad_mesh = kernel(
        return_grads,
        shape((1, nodes, width), F32),
        [pltpu.VMEM((half // LANES, halves, LANES), F32)],
        10**9,
    )(
        arrived,
        mesh_rows,
        send_grad,
        recv_grad,
        a_send,
        a_recv,
        cotangent,
    )
    return (mesh_out, grad_mesh, grad_weights)


def solution(mesh):
    torus = Mesh(
        mesh.devices.reshape(8, 8, 2, mesh.shape["sample"]),
        ("graph_0", "graph_1", "graph_2", "sample"),
    )
    in_specs = (
        P("sample", GRAPH, None),
        P("sample", GRAPH, None),
        P(None, GRAPH),
        P(),
        P(),
        P(),
        P(),
        P(),
        P(),
        P("sample", GRAPH, None),
        P(GRAPH, None, None),
        P(GRAPH, None),
        P(GRAPH),
        P(GRAPH),
        P(GRAPH, None, None),
        P(GRAPH),
        P(GRAPH),
    )
    out_specs = (P("sample", GRAPH, None), P("sample", GRAPH, None), P(GRAPH, None))
    return jax.shard_map(
        on_device, mesh=torus, in_specs=in_specs, out_specs=out_specs, check_vma=False
    )
```

```python
import functools

import jax
import jax.numpy as jnp
from jax import lax
from jax.experimental import pallas as pl
from jax.experimental.pallas import tpu as pltpu
from jax.sharding import Mesh
from jax.sharding import PartitionSpec as P

GRAPH = ("graph_0", "graph_1", "graph_2")
LANES = 128
F32 = jnp.float32
BF16 = jnp.bfloat16
GRANTS = (60, 40, 40)


def dot(left, right):
    return jnp.dot(left, right, preferred_element_type=F32)


def times_transposed(left, right):
    return lax.dot_general(left, right, (((1,), (1,)), ((), ())), preferred_element_type=F32)


def inner_rows(left, right):
    return lax.dot_general(left, right, (((0,), (0,)), ((), ())), preferred_element_type=F32)


def logistic(v):
    return 1.0 / (1.0 + jnp.exp(-v))


def silu(v):
    return v * logistic(v)


def slope_from(v, s):
    return s * (1.0 + v * (1.0 - s))


def columns_of(row):
    return jnp.transpose(jnp.broadcast_to(row, (LANES, row.shape[1])))


def slot_columns(ids):
    slots, groups = ids.shape
    turned = jnp.transpose(jnp.concatenate([ids] * (LANES // slots), axis=0))
    return [jnp.broadcast_to(turned[:, j : j + 1], (groups, LANES)) for j in range(slots)]


def select_rows(column, size):
    lane = lax.broadcasted_iota(jnp.int32, column.shape, 1)
    blocks = [
        jnp.where(column == lane + LANES * k, 1.0, 0.0).astype(BF16) for k in range(size // LANES)
    ]
    return blocks[0] if len(blocks) == 1 else jnp.concatenate(blocks, axis=1)


def select_columns(row, size):
    segment = lax.broadcasted_iota(jnp.int32, (size, row.shape[1]), 0)
    return jnp.where(segment == row, 1.0, 0.0).astype(BF16)


def strided_store(spread, start, stride, value):
    rows, width = value.shape
    for k in range(width // LANES):
        spread[k, pl.ds(start, rows, stride=stride), :] = value[:, k * LANES : (k + 1) * LANES]


def gather_blocks(spread, out_ref):
    for k in range(spread.shape[0]):
        out_ref[:, k * LANES : (k + 1) * LANES] = spread[k].astype(out_ref.dtype)


def scatter_blocks(spread, in_ref):
    for k in range(spread.shape[0]):
        spread[k] = in_ref[:, k * LANES : (k + 1) * LANES].astype(spread.dtype)


def pick_grid(rows_hbm, counts_hbm, grid_hbm, out_ref, rows, counts, grid, sems, spread):
    copies = [
        pltpu.make_async_copy(source, target, sems.at[i])
        for i, (source, target) in enumerate(
            ((rows_hbm, rows), (counts_hbm, counts), (grid_hbm, grid))
        )
    ]
    for copy in copies:
        copy.start()
    copies[0].wait()
    copies[1].wait()
    slots = rows.shape[1]
    slot = lax.broadcasted_iota(jnp.int32, rows.shape[1:], 0)
    ids = slot_columns(jnp.where(slot < counts[...], rows[0], -1))
    chosen = jnp.concatenate([select_rows(column, grid.shape[1]) for column in ids], axis=0)
    copies[2].wait()
    picked = dot(chosen, grid[0])
    groups = rows.shape[2]
    for j in range(slots):
        strided_store(spread, j, slots, picked[j * groups : (j + 1) * groups])
    gather_blocks(spread, out_ref)


def encode(
    pieces_ref, senders_ref, receivers_ref, geometry_ref, w_embed_ref, w_g2m_ref, w_geo_ref,
    init_ref, send_rows_ref, latent_ref, halo_ref, spread,
):
    edges = senders_ref.shape[1]
    nodes, width = latent_ref.shape
    inputs = geometry_ref.shape[0]
    geometry = geometry_ref[...].astype(F32)
    blank = jnp.zeros((LANES - inputs, edges), F32)
    geometry = jnp.transpose(jnp.concatenate([geometry, blank], axis=0)).astype(BF16)
    blank = jnp.zeros((LANES - inputs, width), F32)
    weights = [w_g2m_ref[...].astype(F32), w_geo_ref[...].astype(F32), blank]
    weights = jnp.concatenate(weights, axis=0).astype(BF16)
    chosen = select_rows(columns_of(senders_ref[...]), pieces_ref.shape[0])
    raw = dot(chosen, pieces_ref[...]).astype(BF16)
    embedded = silu(dot(raw, w_embed_ref[...])).astype(BF16)
    message = silu(dot(jnp.concatenate([embedded, geometry], axis=1), weights)).astype(BF16)
    gather = select_columns(receivers_ref[...], nodes)
    total = init_ref[0].astype(F32) + dot(gather, message)
    latent = total.astype(BF16)
    latent_ref[...] = latent
    ids = slot_columns(send_rows_ref[0])
    picked = dot(jnp.concatenate([select_rows(column, nodes) for column in ids], axis=0), latent)
    groups = send_rows_ref.shape[2]
    for j in range(len(ids)):
        split_store(spread, j, len(ids), picked[j * groups : (j + 1) * groups])
    gather_blocks(spread, halo_ref)


def split_store(spread, j, slots, value):
    groups, width = value.shape
    strided_store(spread, j, 2 * slots, value[:, : width // 2])
    strided_store(spread, slots + j, 2 * slots, value[:, width // 2 :])


def split_load(spread, j, slots, groups):
    blocks = [
        spread[k, pl.ds(start, groups, stride=2 * slots), :]
        for start in (j, slots + j)
        for k in range(spread.shape[0])
    ]
    return jnp.concatenate(blocks, axis=1)


def weight_grads(
    mine, sibling_ref, table_ref, send_grad_ref, latent_ref, recv_grad_ref, aggregate_ref,
    d_update_ref, out_ref,
):
    half = out_ref.shape[1]
    width = latent_ref.shape[1]
    core = 1 - sibling_ref[0] if mine else sibling_ref[0]
    columns = pl.ds(pl.multiple_of(core * half, half), half)
    pairs = ((table_ref, send_grad_ref), (latent_ref, recv_grad_ref), (aggregate_ref, d_update_ref))
    for i, (left, right) in enumerate(pairs):
        product = inner_rows(left[...], right[:, columns])
        out_ref[i * width : (i + 1) * width, :] = product.astype(out_ref.dtype)


def process(
    slots, sibling_ref, halo_ref, latent_ref, senders_ref, receivers_ref, a_send_ref, a_recv_ref, b_node_ref,
    cot_ref,
    out_ref, back_ref, table_ref, send_grad_ref, recv_grad_ref, aggregate_ref, d_update_ref, send_ref,
    spread,
):
    nodes, width = latent_ref.shape
    rows = table_ref.shape[0]
    remote = rows - nodes
    groups = remote // slots
    scatter_blocks(spread, halo_ref)
    for j in range(slots):
        table_ref[j * groups : (j + 1) * groups, :] = split_load(spread, j, slots, groups).astype(BF16)
    latent = latent_ref[...]
    table_ref[remote:, :] = latent
    ids = senders_ref[...]
    ids = jnp.where(ids < remote, lax.rem(ids, slots) * groups + lax.div(ids, slots), ids)
    receivers = receivers_ref[...]
    receive = select_rows(columns_of(receivers), nodes)
    gather = select_columns(receivers, nodes)
    sent = dot(select_rows(columns_of(ids), rows), table_ref[...]).astype(BF16)
    own = dot(receive, latent).astype(BF16)
    weights = jnp.concatenate([a_send_ref[...], a_recv_ref[...]], axis=0)
    pre_act = dot(jnp.concatenate([sent, own], axis=1), weights)
    gate = logistic(pre_act)
    aggregate = dot(gather, (pre_act * gate).astype(BF16)).astype(BF16)
    aggregate_ref[...] = aggregate
    update = dot(aggregate, b_node_ref[...])
    update_gate = logistic(update)
    out_ref[0] = (latent.astype(F32) + update * update_gate).astype(BF16)
    d_update = (cot_ref[0].astype(F32) * slope_from(update, update_gate)).astype(BF16)
    d_update_ref[...] = d_update
    d_aggregate = times_transposed(d_update, b_node_ref[...]).astype(BF16)
    d_pre = (dot(receive, d_aggregate) * slope_from(pre_act, gate)).astype(BF16)
    sums = dot(jnp.concatenate([select_columns(ids, rows), gather], axis=0), d_pre)
    recv_grad_ref[...] = sums[rows:].astype(BF16)
    send_grad = sums[:rows]
    send_grad_ref[...] = send_grad.astype(BF16)
    for j in range(slots):
        split_store(spread, j, slots, send_grad[j * groups : (j + 1) * groups])
    gather_blocks(spread, back_ref)
    weight_grads(
        False, sibling_ref, table_ref, send_grad_ref, latent_ref, recv_grad_ref, aggregate_ref,
        d_update_ref, send_ref,
    )


def keep_grads(
    sibling_ref, table_ref, send_grad_ref, latent_ref, recv_grad_ref, aggregate_ref, d_update_ref,
    a_send_ref, a_recv_ref, cot_ref, keep_ref, local_ref,
):
    weight_grads(
        True, sibling_ref, table_ref, send_grad_ref, latent_ref, recv_grad_ref, aggregate_ref,
        d_update_ref, keep_ref,
    )
    nodes = latent_ref.shape[0]
    own_rows = send_grad_ref[send_grad_ref.shape[0] - nodes :, :]
    local_ref[...] = (
        cot_ref[0].astype(F32)
        + times_transposed(recv_grad_ref[...], a_recv_ref[...])
        + times_transposed(own_rows, a_send_ref[...])
    )


def pack(keep_ref, other_ref, back_ref, out_ref):
    chips, _, half = keep_ref.shape
    tile = back_ref.shape[2]
    out_ref[:, :, :, :half] = back_ref[...]
    for i in range(3):
        rows = slice(i * tile, (i + 1) * tile)
        total = keep_ref[:, rows, :] + other_ref[:, rows, :].astype(F32)
        if i != 1:
            out_ref[:, i // 2, :, half : 2 * half] = total.astype(BF16)
            continue
        flat = total.reshape(chips * tile, half)
        left, right = flat[:, :LANES], flat[:, LANES:]
        upper = lax.rem(lax.broadcasted_iota(jnp.int32, left.shape, 0), tile) < tile // 2
        first = jnp.where(upper, left, pltpu.roll(right, tile // 2, 0))
        second = jnp.where(upper, pltpu.roll(left, chips * tile - tile // 2, 0), right)
        out_ref[:, 0, :, 2 * half :] = first.astype(BF16).reshape(chips, tile, LANES)
        out_ref[:, 1, :, 2 * half :] = second.astype(BF16).reshape(chips, tile, LANES)


def add_chips(arrived_ref, out_ref):
    chips = arrived_ref.shape[0]
    skip = arrived_ref.shape[3] - out_ref.shape[3]
    total = arrived_ref[0, :, :, skip:].astype(F32)
    for i in range(1, chips):
        total = total + arrived_ref[i, :, :, skip:].astype(F32)
    for i in range(out_ref.shape[0]):
        out_ref[i] = total


def add_samples(sibling_ref, arrived_ref, out_ref):
    total = arrived_ref[0]
    for i in range(1, arrived_ref.shape[0]):
        total = total + arrived_ref[i]
    tile = total.shape[1]
    half = out_ref.shape[1] // 2
    extra = tile // 2
    whole = jnp.concatenate([total[h, :, :half] for h in range(2)], axis=1)
    parts = [total[h, k * extra : (k + 1) * extra, half:] for h in range(2) for k in range(2)]
    middle = jnp.concatenate(parts, axis=1)

    @pl.when(sibling_ref[0] == 1)
    def _():
        out_ref[:tile, :] = whole
        out_ref[tile:, :] = middle

    @pl.when(sibling_ref[0] == 0)
    def _():
        out_ref[:extra, :] = middle
        out_ref[extra:, :] = whole


def return_grads(back_ref, send_rows_ref, a_send_ref, local_ref, out_ref, spread):
    nodes = local_ref.shape[0]
    slots, groups = send_rows_ref.shape[1:]
    scatter_blocks(spread, back_ref)
    wanted = send_rows_ref[0]
    arrived = [split_load(spread, j, slots, groups).astype(BF16) for j in range(slots)]
    chosen = [select_columns(wanted[j : j + 1], nodes) for j in range(slots)]
    total = dot(jnp.concatenate(chosen, axis=1), jnp.concatenate(arrived, axis=0))
    high = total.astype(BF16)
    rest = total - high.astype(F32)
    low = rest.astype(BF16)
    a_send = a_send_ref[...]
    out_ref[0] = local_ref[...] + (times_transposed(high, a_send) + times_transposed(low, a_send))


def finish(
    sibling_ref, copies_ref, back_ref, send_rows_ref, a_send_ref, local_ref, weights_ref, mesh_ref,
    spread,
):
    add_samples(sibling_ref, copies_ref, weights_ref)
    return_grads(back_ref, send_rows_ref, a_send_ref, local_ref, mesh_ref, spread)


def shape(dims, dtype):
    return jax.ShapeDtypeStruct(dims, dtype)


def kernel(body, outs, scratch, flops, first=0, space=None, grant=24):
    def call(*operands):
        specs = [
            pl.BlockSpec(memory_space=space if i < first else pltpu.VMEM)
            for i in range(len(operands))
        ]
        moved = sum(x.size * x.dtype.itemsize for x in operands)
        return pl.pallas_call(
            body,
            out_shape=outs,
            in_specs=specs,
            out_specs=jax.tree.map(lambda _: pl.BlockSpec(memory_space=pltpu.VMEM), outs),
            scratch_shapes=scratch,
            compiler_params=pltpu.CompilerParams(vmem_limit_bytes=grant << 20),
            cost_estimate=pl.CostEstimate(flops=flops, bytes_accessed=moved, transcendentals=0),
        )(*operands)

    return call


def exchange(x, axis):
    return lax.all_to_all(x, axis, split_axis=0, concat_axis=0, tiled=True)


def share(keep, send, back, core):
    half = keep.shape[1]
    tile = 8
    chips = lax.axis_size("graph_0") * lax.axis_size("graph_1")
    samples = lax.axis_size("sample")
    lanes = 2 * half + half // 2
    other = lax.ppermute(send, "graph_2", [(0, 1), (1, 0)])
    packed = kernel(pack, shape((chips, 2, tile, lanes), BF16), [], 10**7)(
        keep.reshape(chips, -1, half),
        other.reshape(chips, -1, half),
        back.reshape(chips, 2, tile, half),
    )
    arrived = exchange(packed.reshape(2 * chips, tile, lanes), GRAPH)
    copies = kernel(add_chips, shape((samples, 2, tile, lanes - half), F32), [], 10**7)(
        arrived.reshape(chips, 2, tile, lanes)
    )
    copies = exchange(copies, "sample")
    copies, core = lax.optimization_barrier((copies, core))
    return arrived.reshape(2 * chips * tile, lanes), copies, 1 - core


def on_device(
    grid_in,
    mesh_init,
    g2m_geometry,
    w_embed,
    w_g2m,
    w_geo,
    a_send,
    a_recv,
    b_node,
    cotangent,
    g2m_send_rows,
    g2m_counts,
    g2m_senders,
    g2m_receivers,
    mesh_send_rows,
    mesh_senders,
    mesh_receivers,
):
    groups, slots = g2m_send_rows.shape[1:]
    halo_slots = mesh_send_rows.shape[2]
    features = grid_in.shape[2]
    width = w_g2m.shape[1]
    half = width // 2
    nodes = mesh_init.shape[1]
    table_rows = groups * halo_slots + nodes
    halves = 2 * groups * halo_slots

    core = lax.axis_index("graph_2").astype(jnp.int32)[None]
    core, g2m_counts = lax.optimization_barrier((core, g2m_counts))
    grid_rows = jnp.transpose(g2m_send_rows, (0, 2, 1))
    mesh_rows = jnp.transpose(mesh_send_rows, (0, 2, 1))
    raw_rows = kernel(
        pick_grid,
        shape((groups * slots, features), BF16),
        [
            pltpu.VMEM(grid_rows.shape, jnp.int32),
            pltpu.VMEM(g2m_counts.shape, jnp.int32),
            pltpu.VMEM(grid_in.shape, BF16),
            pltpu.SemaphoreType.DMA((3,)),
            pltpu.VMEM((features // LANES, groups * slots, LANES), F32),
        ],
        10**8,
        3,
        pltpu.HBM,
        GRANTS[0],
    )(grid_rows, g2m_counts, grid_in)
    pieces = exchange(raw_rows.reshape(groups, slots, features), GRAPH)

    latent, halo = kernel(
        encode,
        (shape((nodes, width), BF16), shape((halves, half), BF16)),
        [pltpu.VMEM((half // LANES, halves, LANES), F32)],
        2 * 10**9,
        grant=GRANTS[1],
    )(
        pieces.reshape(groups * slots, features),
        g2m_senders[None],
        g2m_receivers[None],
        g2m_geometry,
        w_embed,
        w_g2m,
        w_geo,
        mesh_init,
        mesh_rows,
    )
    halo = exchange(halo.reshape(groups, 2 * halo_slots, half), GRAPH)
    halo, core = lax.optimization_barrier((halo, core))
    sibling = 1 - core

    mesh_out, back, table, send_grad, recv_grad, aggregate, d_update, send = kernel(
        functools.partial(process, halo_slots),
        (
            shape((1, nodes, width), BF16),
            shape((halves, half), BF16),
            shape((table_rows, width), BF16),
            shape((table_rows, width), BF16),
            shape((nodes, width), BF16),
            shape((nodes, width), BF16),
            shape((nodes, width), BF16),
            shape((3 * width, half), BF16),
        ),
        [pltpu.VMEM((half // LANES, halves, LANES), F32)],
        3 * 10**9,
        1,
        pltpu.SMEM,
        GRANTS[2],
    )(
        sibling,
        halo.reshape(halves, half),
        latent,
        mesh_senders[None],
        mesh_receivers[None],
        a_send,
        a_recv,
        b_node,
        cotangent,
    )

    operands = (table, send_grad, latent, recv_grad, aggregate, d_update)
    keep, local = kernel(
        keep_grads,
        (shape((3 * width, half), F32), shape((nodes, width), F32)),
        [],
        7 * 10**8,
        1,
        pltpu.SMEM,
    )(sibling, *operands, a_send, a_recv, cotangent)
    arrived, copies, sibling = share(keep, send, back, core)
    grad_weights, grad_mesh = kernel(
        finish,
        (shape((3 * width // groups, width), F32), shape((1, nodes, width), F32)),
        [pltpu.VMEM((half // LANES, halves, LANES), F32)],
        10**9,
        1,
        pltpu.SMEM,
    )(sibling, copies, arrived, mesh_rows, a_send, local)
    return (mesh_out, grad_mesh, grad_weights)


def solution(mesh):
    torus = Mesh(
        mesh.devices.reshape(8, 8, 2, mesh.shape["sample"]),
        ("graph_0", "graph_1", "graph_2", "sample"),
    )
    in_specs = (
        P("sample", GRAPH, None),
        P("sample", GRAPH, None),
        P(None, GRAPH),
        P(),
        P(),
        P(),
        P(),
        P(),
        P(),
        P("sample", GRAPH, None),
        P(GRAPH, None, None),
        P(GRAPH, None),
        P(GRAPH),
        P(GRAPH),
        P(GRAPH, None, None),
        P(GRAPH),
        P(GRAPH),
    )
    out_specs = (P("sample", GRAPH, None), P("sample", GRAPH, None), P(GRAPH, None))
    return jax.shard_map(
        on_device, mesh=torus, in_specs=in_specs, out_specs=out_specs, check_vma=False
    )
```

```python
import functools

import jax
import jax.numpy as jnp
from jax import lax
from jax.experimental import pallas as pl
from jax.experimental.pallas import tpu as pltpu
from jax.sharding import Mesh
from jax.sharding import PartitionSpec as P

GRAPH = ("graph_0", "graph_1", "graph_2")
LANES = 128
F32 = jnp.float32
BF16 = jnp.bfloat16
GRANTS = (60, 40, 40)


def dot(left, right):
    return jnp.dot(left, right, preferred_element_type=F32)


def times_transposed(left, right):
    return lax.dot_general(left, right, (((1,), (1,)), ((), ())), preferred_element_type=F32)


def inner_rows(left, right):
    return lax.dot_general(left, right, (((0,), (0,)), ((), ())), preferred_element_type=F32)


def logistic(v):
    return 1.0 / (1.0 + jnp.exp(-v))


def silu(v):
    return v * logistic(v)


def slope_from(v, s):
    return s * (1.0 + v * (1.0 - s))


def columns_of(row):
    return jnp.transpose(jnp.broadcast_to(row, (LANES, row.shape[1])))


def slot_columns(ids):
    slots, groups = ids.shape
    turned = jnp.transpose(jnp.concatenate([ids] * (LANES // slots), axis=0))
    return [jnp.broadcast_to(turned[:, j : j + 1], (groups, LANES)) for j in range(slots)]


def select_rows(column, size):
    lane = lax.broadcasted_iota(jnp.int32, column.shape, 1)
    blocks = [
        jnp.where(column == lane + LANES * k, 1.0, 0.0).astype(BF16) for k in range(size // LANES)
    ]
    return blocks[0] if len(blocks) == 1 else jnp.concatenate(blocks, axis=1)


def select_columns(row, size):
    segment = lax.broadcasted_iota(jnp.int32, (size, row.shape[1]), 0)
    return jnp.where(segment == row, 1.0, 0.0).astype(BF16)


def strided_store(spread, start, stride, value):
    rows, width = value.shape
    for k in range(width // LANES):
        spread[k, pl.ds(start, rows, stride=stride), :] = value[:, k * LANES : (k + 1) * LANES]


def gather_blocks(spread, out_ref):
    for k in range(spread.shape[0]):
        out_ref[:, k * LANES : (k + 1) * LANES] = spread[k].astype(out_ref.dtype)


def scatter_blocks(spread, in_ref):
    for k in range(spread.shape[0]):
        spread[k] = in_ref[:, k * LANES : (k + 1) * LANES].astype(spread.dtype)


def pick_grid(rows_hbm, counts_hbm, grid_hbm, out_ref, rows, counts, grid, sems, spread):
    copies = [
        pltpu.make_async_copy(source, target, sems.at[i])
        for i, (source, target) in enumerate(
            ((rows_hbm, rows), (counts_hbm, counts), (grid_hbm, grid))
        )
    ]
    for copy in copies:
        copy.start()
    copies[0].wait()
    copies[1].wait()
    slots = rows.shape[1]
    slot = lax.broadcasted_iota(jnp.int32, rows.shape[1:], 0)
    ids = slot_columns(jnp.where(slot < counts[...], rows[0], -1))
    chosen = jnp.concatenate([select_rows(column, grid.shape[1]) for column in ids], axis=0)
    copies[2].wait()
    picked = dot(chosen, grid[0])
    groups = rows.shape[2]
    for j in range(slots):
        strided_store(spread, j, slots, picked[j * groups : (j + 1) * groups])
    gather_blocks(spread, out_ref)


def encode(
    pieces_ref, senders_ref, receivers_ref, geometry_ref, w_embed_ref, w_g2m_ref, w_geo_ref,
    init_ref, send_rows_ref, latent_ref, halo_ref, spread,
):
    edges = senders_ref.shape[1]
    nodes, width = latent_ref.shape
    inputs = geometry_ref.shape[0]
    geometry = geometry_ref[...].astype(F32)
    blank = jnp.zeros((LANES - inputs, edges), F32)
    geometry = jnp.transpose(jnp.concatenate([geometry, blank], axis=0)).astype(BF16)
    blank = jnp.zeros((LANES - inputs, width), F32)
    weights = [w_g2m_ref[...].astype(F32), w_geo_ref[...].astype(F32), blank]
    weights = jnp.concatenate(weights, axis=0).astype(BF16)
    chosen = select_rows(columns_of(senders_ref[...]), pieces_ref.shape[0])
    raw = dot(chosen, pieces_ref[...]).astype(BF16)
    embedded = silu(dot(raw, w_embed_ref[...])).astype(BF16)
    message = silu(dot(jnp.concatenate([embedded, geometry], axis=1), weights)).astype(BF16)
    gather = select_columns(receivers_ref[...], nodes)
    total = init_ref[0].astype(F32) + dot(gather, message)
    latent = total.astype(BF16)
    latent_ref[...] = latent
    ids = slot_columns(send_rows_ref[0])
    picked = dot(jnp.concatenate([select_rows(column, nodes) for column in ids], axis=0), latent)
    groups = send_rows_ref.shape[2]
    for j in range(len(ids)):
        split_store(spread, j, len(ids), picked[j * groups : (j + 1) * groups])
    gather_blocks(spread, halo_ref)


def split_store(spread, j, slots, value):
    groups, width = value.shape
    strided_store(spread, j, 2 * slots, value[:, : width // 2])
    strided_store(spread, slots + j, 2 * slots, value[:, width // 2 :])


def split_load(spread, j, slots, groups):
    blocks = [
        spread[k, pl.ds(start, groups, stride=2 * slots), :]
        for start in (j, slots + j)
        for k in range(spread.shape[0])
    ]
    return jnp.concatenate(blocks, axis=1)


def weight_grads(
    mine, sibling_ref, table_ref, send_grad_ref, latent_ref, recv_grad_ref, aggregate_ref,
    d_update_ref, out_ref,
):
    half = out_ref.shape[1]
    width = latent_ref.shape[1]
    core = 1 - sibling_ref[0] if mine else sibling_ref[0]
    columns = pl.ds(pl.multiple_of(core * half, half), half)
    pairs = ((table_ref, send_grad_ref), (latent_ref, recv_grad_ref), (aggregate_ref, d_update_ref))
    for i, (left, right) in enumerate(pairs):
        product = inner_rows(left[...], right[:, columns])
        out_ref[i * width : (i + 1) * width, :] = product.astype(out_ref.dtype)


def process(
    slots, sibling_ref, halo_ref, latent_ref, senders_ref, receivers_ref, a_send_ref, a_recv_ref, b_node_ref,
    cot_ref,
    out_ref, back_ref, table_ref, send_grad_ref, recv_grad_ref, aggregate_ref, d_update_ref, send_ref,
    spread,
):
    nodes, width = latent_ref.shape
    rows = table_ref.shape[0]
    remote = rows - nodes
    groups = remote // slots
    scatter_blocks(spread, halo_ref)
    for j in range(slots):
        table_ref[j * groups : (j + 1) * groups, :] = split_load(spread, j, slots, groups).astype(BF16)
    latent = latent_ref[...]
    table_ref[remote:, :] = latent
    ids = senders_ref[...]
    ids = jnp.where(ids < remote, lax.rem(ids, slots) * groups + lax.div(ids, slots), ids)
    receivers = receivers_ref[...]
    receive = select_rows(columns_of(receivers), nodes)
    gather = select_columns(receivers, nodes)
    sent = dot(select_rows(columns_of(ids), rows), table_ref[...]).astype(BF16)
    own = dot(receive, latent).astype(BF16)
    weights = jnp.concatenate([a_send_ref[...], a_recv_ref[...]], axis=0)
    pre_act = dot(jnp.concatenate([sent, own], axis=1), weights)
    gate = logistic(pre_act)
    aggregate = dot(gather, (pre_act * gate).astype(BF16)).astype(BF16)
    aggregate_ref[...] = aggregate
    update = dot(aggregate, b_node_ref[...])
    update_gate = logistic(update)
    out_ref[0] = (latent.astype(F32) + update * update_gate).astype(BF16)
    d_update = (cot_ref[0].astype(F32) * slope_from(update, update_gate)).astype(BF16)
    d_update_ref[...] = d_update
    d_aggregate = times_transposed(d_update, b_node_ref[...]).astype(BF16)
    d_pre = (dot(receive, d_aggregate) * slope_from(pre_act, gate)).astype(BF16)
    sums = dot(jnp.concatenate([select_columns(ids, rows), gather], axis=0), d_pre)
    recv_grad_ref[...] = sums[rows:].astype(BF16)
    send_grad = sums[:rows]
    send_grad_ref[...] = send_grad.astype(BF16)
    for j in range(slots):
        split_store(spread, j, slots, send_grad[j * groups : (j + 1) * groups])
    gather_blocks(spread, back_ref)
    weight_grads(
        False, sibling_ref, table_ref, send_grad_ref, latent_ref, recv_grad_ref, aggregate_ref,
        d_update_ref, send_ref,
    )


def keep_grads(
    sibling_ref, table_ref, send_grad_ref, latent_ref, recv_grad_ref, aggregate_ref, d_update_ref,
    a_send_ref, a_recv_ref, cot_ref, keep_ref, local_ref,
):
    weight_grads(
        True, sibling_ref, table_ref, send_grad_ref, latent_ref, recv_grad_ref, aggregate_ref,
        d_update_ref, keep_ref,
    )
    nodes = latent_ref.shape[0]
    own_rows = send_grad_ref[send_grad_ref.shape[0] - nodes :, :]
    local_ref[...] = (
        cot_ref[0].astype(F32)
        + times_transposed(recv_grad_ref[...], a_recv_ref[...])
        + times_transposed(own_rows, a_send_ref[...])
    )


def pack(keep_ref, other_ref, back_ref, out_ref):
    half = keep_ref.shape[2]
    tile = back_ref.shape[2]
    for i in range(2):
        out_ref[:, :, i * half : (i + 1) * half] = back_ref[:, i]
    for i in range(3):
        rows = slice(i * tile, (i + 1) * tile)
        total = keep_ref[:, rows, :] + other_ref[:, rows, :].astype(F32)
        out_ref[:, :, (2 + i) * half : (3 + i) * half] = total.astype(BF16)


def add_chips(sibling_ref, arrived_ref, copies_ref, theirs_ref):
    samples, _, rows, half = copies_ref.shape
    tile = rows // 2
    columns = pl.ds(pl.multiple_of(sibling_ref[0] * half, half), half)
    theirs_ref[...] = arrived_ref[:, columns]
    total = arrived_ref[:tile, 2 * half :].astype(F32)
    for i in range(1, arrived_ref.shape[0] // tile):
        total = total + arrived_ref[i * tile : (i + 1) * tile, 2 * half :].astype(F32)
    tiles = [total[:, i * half : (i + 1) * half] for i in range(3)]
    for i in range(samples):
        for core in range(2):
            copies_ref[i, core, :tile, :] = tiles[core]
            copies_ref[i, core, tile:, :] = tiles[core + 1]


def add_samples(sibling_ref, arrived_ref, out_ref):
    total = arrived_ref[0]
    for i in range(1, arrived_ref.shape[0]):
        total = total + arrived_ref[i]
    whole = jnp.concatenate([total[0], total[1]], axis=1)
    rows = out_ref.shape[0]

    @pl.when(sibling_ref[0] == 1)
    def _():
        out_ref[...] = whole[:rows]

    @pl.when(sibling_ref[0] == 0)
    def _():
        out_ref[...] = whole[whole.shape[0] - rows :]


def interleave(sibling_ref, arrived_ref, other_ref, spread):
    half = other_ref.shape[1]
    tile = 8
    columns = pl.ds(pl.multiple_of((1 - sibling_ref[0]) * half, half), half)
    mine = arrived_ref[:, columns].astype(F32)
    other = other_ref[...].astype(F32)
    first = sibling_ref[0] == 1
    pair = jnp.where(first, mine, other), jnp.where(first, other, mine)
    for k in range(spread.shape[0]):
        lanes = slice(k * LANES, (k + 1) * LANES)
        parts = [part[:, lanes].reshape(-1, 1, tile, LANES) for part in pair]
        spread[k] = jnp.concatenate(parts, axis=1).reshape(-1, LANES)


def return_grads(send_rows_ref, a_send_ref, local_ref, out_ref, spread):
    nodes = local_ref.shape[0]
    slots, groups = send_rows_ref.shape[1:]
    wanted = send_rows_ref[0]
    arrived = [split_load(spread, j, slots, groups).astype(BF16) for j in range(slots)]
    chosen = [select_columns(wanted[j : j + 1], nodes) for j in range(slots)]
    total = dot(jnp.concatenate(chosen, axis=1), jnp.concatenate(arrived, axis=0))
    high = total.astype(BF16)
    rest = total - high.astype(F32)
    low = rest.astype(BF16)
    a_send = a_send_ref[...]
    out_ref[0] = local_ref[...] + (times_transposed(high, a_send) + times_transposed(low, a_send))


def finish(
    sibling_ref, copies_ref, arrived_ref, other_ref, send_rows_ref, a_send_ref, local_ref,
    weights_ref, mesh_ref, spread,
):
    add_samples(sibling_ref, copies_ref, weights_ref)
    interleave(sibling_ref, arrived_ref, other_ref, spread)
    return_grads(send_rows_ref, a_send_ref, local_ref, mesh_ref, spread)


def shape(dims, dtype):
    return jax.ShapeDtypeStruct(dims, dtype)


def kernel(body, outs, scratch, flops, first=0, space=None, grant=24):
    def call(*operands):
        specs = [
            pl.BlockSpec(memory_space=space if i < first else pltpu.VMEM)
            for i in range(len(operands))
        ]
        moved = sum(x.size * x.dtype.itemsize for x in operands)
        return pl.pallas_call(
            body,
            out_shape=outs,
            in_specs=specs,
            out_specs=jax.tree.map(lambda _: pl.BlockSpec(memory_space=pltpu.VMEM), outs),
            scratch_shapes=scratch,
            compiler_params=pltpu.CompilerParams(vmem_limit_bytes=grant << 20),
            cost_estimate=pl.CostEstimate(flops=flops, bytes_accessed=moved, transcendentals=0),
        )(*operands)

    return call


def exchange(x, axis):
    return lax.all_to_all(x, axis, split_axis=0, concat_axis=0, tiled=True)


def share(keep, send, back, core):
    half = keep.shape[1]
    tile = 8
    chips = lax.axis_size("graph_0") * lax.axis_size("graph_1")
    samples = lax.axis_size("sample")
    swap = [(0, 1), (1, 0)]
    other = lax.ppermute(send, "graph_2", swap)
    packed = kernel(pack, shape((chips, tile, 5 * half), BF16), [], 10**7)(
        keep.reshape(chips, -1, half),
        other.reshape(chips, -1, half),
        back.reshape(chips, 2, tile, half),
    )
    arrived = exchange(packed, ("graph_0", "graph_1"))
    arrived, core = lax.optimization_barrier((arrived.reshape(chips * tile, 5 * half), core))
    sibling = 1 - core
    copies, theirs = kernel(
        add_chips,
        (shape((samples, 2, 2 * tile, half), F32), shape((chips * tile, half), BF16)),
        [],
        10**7,
        1,
        pltpu.SMEM,
    )(sibling, arrived)
    theirs = lax.ppermute(theirs, "graph_2", swap)
    copies = exchange(copies.reshape(2 * samples, 2 * tile, half), ("sample", "graph_2"))
    return arrived, theirs, copies.reshape(samples, 2, 2 * tile, half), sibling


def on_device(
    grid_in,
    mesh_init,
    g2m_geometry,
    w_embed,
    w_g2m,
    w_geo,
    a_send,
    a_recv,
    b_node,
    cotangent,
    g2m_send_rows,
    g2m_counts,
    g2m_senders,
    g2m_receivers,
    mesh_send_rows,
    mesh_senders,
    mesh_receivers,
):
    groups, slots = g2m_send_rows.shape[1:]
    halo_slots = mesh_send_rows.shape[2]
    features = grid_in.shape[2]
    width = w_g2m.shape[1]
    half = width // 2
    nodes = mesh_init.shape[1]
    table_rows = groups * halo_slots + nodes
    halves = 2 * groups * halo_slots

    core = lax.axis_index("graph_2").astype(jnp.int32)[None]
    core, g2m_counts = lax.optimization_barrier((core, g2m_counts))
    grid_rows = jnp.transpose(g2m_send_rows, (0, 2, 1))
    mesh_rows = jnp.transpose(mesh_send_rows, (0, 2, 1))
    raw_rows = kernel(
        pick_grid,
        shape((groups * slots, features), BF16),
        [
            pltpu.VMEM(grid_rows.shape, jnp.int32),
            pltpu.VMEM(g2m_counts.shape, jnp.int32),
            pltpu.VMEM(grid_in.shape, BF16),
            pltpu.SemaphoreType.DMA((3,)),
            pltpu.VMEM((features // LANES, groups * slots, LANES), F32),
        ],
        10**8,
        3,
        pltpu.HBM,
        GRANTS[0],
    )(grid_rows, g2m_counts, grid_in)
    pieces = exchange(raw_rows.reshape(groups, slots, features), GRAPH)

    latent, halo = kernel(
        encode,
        (shape((nodes, width), BF16), shape((halves, half), BF16)),
        [pltpu.VMEM((half // LANES, halves, LANES), F32)],
        2 * 10**9,
        grant=GRANTS[1],
    )(
        pieces.reshape(groups * slots, features),
        g2m_senders[None],
        g2m_receivers[None],
        g2m_geometry,
        w_embed,
        w_g2m,
        w_geo,
        mesh_init,
        mesh_rows,
    )
    halo = exchange(halo.reshape(groups, 2 * halo_slots, half), GRAPH)
    halo, core = lax.optimization_barrier((halo, core))
    sibling = 1 - core

    mesh_out, back, table, send_grad, recv_grad, aggregate, d_update, send = kernel(
        functools.partial(process, halo_slots),
        (
            shape((1, nodes, width), BF16),
            shape((halves, half), BF16),
            shape((table_rows, width), BF16),
            shape((table_rows, width), BF16),
            shape((nodes, width), BF16),
            shape((nodes, width), BF16),
            shape((nodes, width), BF16),
            shape((3 * width, half), BF16),
        ),
        [pltpu.VMEM((half // LANES, halves, LANES), F32)],
        3 * 10**9,
        1,
        pltpu.SMEM,
        GRANTS[2],
    )(
        sibling,
        halo.reshape(halves, half),
        latent,
        mesh_senders[None],
        mesh_receivers[None],
        a_send,
        a_recv,
        b_node,
        cotangent,
    )

    operands = (table, send_grad, latent, recv_grad, aggregate, d_update)
    keep, local = kernel(
        keep_grads,
        (shape((3 * width, half), F32), shape((nodes, width), F32)),
        [],
        7 * 10**8,
        1,
        pltpu.SMEM,
    )(sibling, *operands, a_send, a_recv, cotangent)
    arrived, theirs, copies, sibling = share(keep, send, back, core)
    grad_weights, grad_mesh = kernel(
        finish,
        (shape((3 * width // groups, width), F32), shape((1, nodes, width), F32)),
        [pltpu.VMEM((half // LANES, halves, LANES), F32)],
        10**9,
        1,
        pltpu.SMEM,
    )(sibling, copies, arrived, theirs, mesh_rows, a_send, local)
    return (mesh_out, grad_mesh, grad_weights)


def solution(mesh):
    torus = Mesh(
        mesh.devices.reshape(8, 8, 2, mesh.shape["sample"]),
        ("graph_0", "graph_1", "graph_2", "sample"),
    )
    in_specs = (
        P("sample", GRAPH, None),
        P("sample", GRAPH, None),
        P(None, GRAPH),
        P(),
        P(),
        P(),
        P(),
        P(),
        P(),
        P("sample", GRAPH, None),
        P(GRAPH, None, None),
        P(GRAPH, None),
        P(GRAPH),
        P(GRAPH),
        P(GRAPH, None, None),
        P(GRAPH),
        P(GRAPH),
    )
    out_specs = (P("sample", GRAPH, None), P("sample", GRAPH, None), P(GRAPH, None))
    return jax.shard_map(
        on_device, mesh=torus, in_specs=in_specs, out_specs=out_specs, check_vma=False
    )
```

```python
import functools

import jax
import jax.numpy as jnp
from jax import lax
from jax.experimental import pallas as pl
from jax.experimental.pallas import tpu as pltpu
from jax.sharding import Mesh
from jax.sharding import PartitionSpec as P

GRAPH = ("graph_0", "graph_1", "graph_2")
LANES = 128
F32 = jnp.float32
BF16 = jnp.bfloat16
GRANTS = (60, 40, 40)


def dot(left, right):
    return jnp.dot(left, right, preferred_element_type=F32)


def times_transposed(left, right):
    return lax.dot_general(left, right, (((1,), (1,)), ((), ())), preferred_element_type=F32)


def inner_rows(left, right):
    return lax.dot_general(left, right, (((0,), (0,)), ((), ())), preferred_element_type=F32)


def logistic(v):
    return 1.0 / (1.0 + jnp.exp(-v))


def silu(v):
    return v * logistic(v)


def slope_from(v, s):
    return s * (1.0 + v * (1.0 - s))


def columns_of(row):
    return jnp.transpose(jnp.broadcast_to(row, (LANES, row.shape[1])))


def slot_columns(ids):
    slots, groups = ids.shape
    turned = jnp.transpose(jnp.concatenate([ids] * (LANES // slots), axis=0))
    return [jnp.broadcast_to(turned[:, j : j + 1], (groups, LANES)) for j in range(slots)]


def select_rows(column, size):
    lane = lax.broadcasted_iota(jnp.int32, column.shape, 1)
    blocks = [
        jnp.where(column == lane + LANES * k, 1.0, 0.0).astype(BF16) for k in range(size // LANES)
    ]
    return blocks[0] if len(blocks) == 1 else jnp.concatenate(blocks, axis=1)


def select_columns(row, size):
    segment = lax.broadcasted_iota(jnp.int32, (size, row.shape[1]), 0)
    return jnp.where(segment == row, 1.0, 0.0).astype(BF16)


def strided_store(spread, start, stride, value):
    rows, width = value.shape
    for k in range(width // LANES):
        spread[k, pl.ds(start, rows, stride=stride), :] = value[:, k * LANES : (k + 1) * LANES]


def gather_blocks(spread, out_ref):
    for k in range(spread.shape[0]):
        out_ref[:, k * LANES : (k + 1) * LANES] = spread[k].astype(out_ref.dtype)


def scatter_blocks(spread, in_ref):
    for k in range(spread.shape[0]):
        spread[k] = in_ref[:, k * LANES : (k + 1) * LANES].astype(spread.dtype)


def pick_grid(rows_hbm, counts_hbm, grid_hbm, out_ref, rows, counts, grid, sems, spread):
    copies = [
        pltpu.make_async_copy(source, target, sems.at[i])
        for i, (source, target) in enumerate(
            ((rows_hbm, rows), (counts_hbm, counts), (grid_hbm, grid))
        )
    ]
    for copy in copies:
        copy.start()
    copies[0].wait()
    copies[1].wait()
    slots = rows.shape[1]
    slot = lax.broadcasted_iota(jnp.int32, rows.shape[1:], 0)
    ids = slot_columns(jnp.where(slot < counts[...], rows[0], -1))
    chosen = jnp.concatenate([select_rows(column, grid.shape[1]) for column in ids], axis=0)
    copies[2].wait()
    picked = dot(chosen, grid[0])
    groups = rows.shape[2]
    for j in range(slots):
        strided_store(spread, j, slots, picked[j * groups : (j + 1) * groups])
    gather_blocks(spread, out_ref)


def encode(
    pieces_ref, senders_ref, receivers_ref, geometry_ref, w_embed_ref, w_g2m_ref, w_geo_ref,
    init_ref, send_rows_ref, latent_ref, halo_ref, spread,
):
    edges = senders_ref.shape[1]
    nodes, width = latent_ref.shape
    inputs = geometry_ref.shape[0]
    geometry = geometry_ref[...].astype(F32)
    blank = jnp.zeros((LANES - inputs, edges), F32)
    geometry = jnp.transpose(jnp.concatenate([geometry, blank], axis=0)).astype(BF16)
    blank = jnp.zeros((LANES - inputs, width), F32)
    weights = [w_g2m_ref[...].astype(F32), w_geo_ref[...].astype(F32), blank]
    weights = jnp.concatenate(weights, axis=0).astype(BF16)
    chosen = select_rows(columns_of(senders_ref[...]), pieces_ref.shape[0])
    raw = dot(chosen, pieces_ref[...]).astype(BF16)
    embedded = silu(dot(raw, w_embed_ref[...])).astype(BF16)
    message = silu(dot(jnp.concatenate([embedded, geometry], axis=1), weights)).astype(BF16)
    gather = select_columns(receivers_ref[...], nodes)
    total = init_ref[0].astype(F32) + dot(gather, message)
    latent = total.astype(BF16)
    latent_ref[...] = latent
    ids = slot_columns(send_rows_ref[0])
    picked = dot(jnp.concatenate([select_rows(column, nodes) for column in ids], axis=0), latent)
    groups = send_rows_ref.shape[2]
    for j in range(len(ids)):
        split_store(spread, j, len(ids), picked[j * groups : (j + 1) * groups])
    gather_blocks(spread, halo_ref)


def split_store(spread, j, slots, value):
    groups, width = value.shape
    strided_store(spread, j, 2 * slots, value[:, : width // 2])
    strided_store(spread, slots + j, 2 * slots, value[:, width // 2 :])


def split_load(spread, j, slots, groups):
    blocks = [
        spread[k, pl.ds(start, groups, stride=2 * slots), :]
        for start in (j, slots + j)
        for k in range(spread.shape[0])
    ]
    return jnp.concatenate(blocks, axis=1)


def weight_grads(
    mine, sibling_ref, table_ref, send_grad_ref, latent_ref, recv_grad_ref, aggregate_ref,
    d_update_ref, out_ref,
):
    half = out_ref.shape[1]
    width = latent_ref.shape[1]
    core = 1 - sibling_ref[0] if mine else sibling_ref[0]
    columns = pl.ds(pl.multiple_of(core * half, half), half)
    pairs = ((table_ref, send_grad_ref), (latent_ref, recv_grad_ref), (aggregate_ref, d_update_ref))
    for i, (left, right) in enumerate(pairs):
        product = inner_rows(left[...], right[:, columns])
        out_ref[i * width : (i + 1) * width, :] = product.astype(out_ref.dtype)


def process(
    slots, halo_ref, latent_ref, senders_ref, receivers_ref, a_send_ref, a_recv_ref, b_node_ref,
    cot_ref,
    out_ref, back_ref, table_ref, send_grad_ref, recv_grad_ref, aggregate_ref, d_update_ref, spread,
):
    nodes, width = latent_ref.shape
    rows = table_ref.shape[0]
    remote = rows - nodes
    groups = remote // slots
    scatter_blocks(spread, halo_ref)
    for j in range(slots):
        table_ref[j * groups : (j + 1) * groups, :] = split_load(spread, j, slots, groups).astype(BF16)
    latent = latent_ref[...]
    table_ref[remote:, :] = latent
    ids = senders_ref[...]
    ids = jnp.where(ids < remote, lax.rem(ids, slots) * groups + lax.div(ids, slots), ids)
    receivers = receivers_ref[...]
    receive = select_rows(columns_of(receivers), nodes)
    gather = select_columns(receivers, nodes)
    sent = dot(select_rows(columns_of(ids), rows), table_ref[...]).astype(BF16)
    own = dot(receive, latent).astype(BF16)
    weights = jnp.concatenate([a_send_ref[...], a_recv_ref[...]], axis=0)
    pre_act = dot(jnp.concatenate([sent, own], axis=1), weights)
    gate = logistic(pre_act)
    aggregate = dot(gather, (pre_act * gate).astype(BF16)).astype(BF16)
    aggregate_ref[...] = aggregate
    update = dot(aggregate, b_node_ref[...])
    update_gate = logistic(update)
    out_ref[0] = (latent.astype(F32) + update * update_gate).astype(BF16)
    d_update = (cot_ref[0].astype(F32) * slope_from(update, update_gate)).astype(BF16)
    d_update_ref[...] = d_update
    d_aggregate = times_transposed(d_update, b_node_ref[...]).astype(BF16)
    d_pre = (dot(receive, d_aggregate) * slope_from(pre_act, gate)).astype(BF16)
    sums = dot(jnp.concatenate([select_columns(ids, rows), gather], axis=0), d_pre)
    recv_grad_ref[...] = sums[rows:].astype(BF16)
    send_grad = sums[:rows]
    send_grad_ref[...] = send_grad.astype(BF16)
    for j in range(slots):
        split_store(spread, j, slots, send_grad[j * groups : (j + 1) * groups])
    gather_blocks(spread, back_ref)


def pack(keep_ref, other_ref, back_ref, out_ref):
    chips, _, half = keep_ref.shape
    tile = back_ref.shape[2]
    out_ref[:, :, :, :half] = back_ref[...]
    for i in range(3):
        rows = slice(i * tile, (i + 1) * tile)
        total = keep_ref[:, rows, :] + other_ref[:, rows, :].astype(F32)
        if i != 1:
            out_ref[:, i // 2, :, half : 2 * half] = total.astype(BF16)
            continue
        flat = total.reshape(chips * tile, half)
        left, right = flat[:, :LANES], flat[:, LANES:]
        upper = lax.rem(lax.broadcasted_iota(jnp.int32, left.shape, 0), tile) < tile // 2
        first = jnp.where(upper, left, pltpu.roll(right, tile // 2, 0))
        second = jnp.where(upper, pltpu.roll(left, chips * tile - tile // 2, 0), right)
        out_ref[:, 0, :, 2 * half :] = first.astype(BF16).reshape(chips, tile, LANES)
        out_ref[:, 1, :, 2 * half :] = second.astype(BF16).reshape(chips, tile, LANES)


def add_chips(arrived_ref, out_ref):
    chips = arrived_ref.shape[0]
    skip = arrived_ref.shape[3] - out_ref.shape[3]
    total = arrived_ref[0, :, :, skip:].astype(F32)
    for i in range(1, chips):
        total = total + arrived_ref[i, :, :, skip:].astype(F32)
    for i in range(out_ref.shape[0]):
        out_ref[i] = total


def add_samples(sibling_ref, arrived_ref, out_ref):
    total = arrived_ref[0]
    for i in range(1, arrived_ref.shape[0]):
        total = total + arrived_ref[i]
    tile = total.shape[1]
    half = out_ref.shape[1] // 2
    extra = tile // 2
    whole = jnp.concatenate([total[h, :, :half] for h in range(2)], axis=1)
    parts = [total[h, k * extra : (k + 1) * extra, half:] for h in range(2) for k in range(2)]
    middle = jnp.concatenate(parts, axis=1)

    @pl.when(sibling_ref[0] == 1)
    def _():
        out_ref[:tile, :] = whole
        out_ref[tile:, :] = middle

    @pl.when(sibling_ref[0] == 0)
    def _():
        out_ref[:extra, :] = middle
        out_ref[extra:, :] = whole


def return_grads(
    back_ref, send_rows_ref, send_grad_ref, recv_grad_ref, a_send_ref, a_recv_ref, cot_ref,
    out_ref, spread,
):
    nodes = recv_grad_ref.shape[0]
    slots, groups = send_rows_ref.shape[1:]
    scatter_blocks(spread, back_ref)
    wanted = send_rows_ref[0]
    arrived = [split_load(spread, j, slots, groups).astype(BF16) for j in range(slots)]
    chosen = [select_columns(wanted[j : j + 1], nodes) for j in range(slots)]
    total = dot(jnp.concatenate(chosen, axis=1), jnp.concatenate(arrived, axis=0))
    total = total + send_grad_ref[slots * groups :, :].astype(F32)
    high = total.astype(BF16)
    rest = total - high.astype(F32)
    low = rest.astype(BF16)
    a_send = a_send_ref[...]
    out_ref[0] = (
        cot_ref[0].astype(F32)
        + times_transposed(recv_grad_ref[...], a_recv_ref[...])
        + (times_transposed(high, a_send) + times_transposed(low, a_send))
    )


def shape(dims, dtype):
    return jax.ShapeDtypeStruct(dims, dtype)


def kernel(body, outs, scratch, flops, first=0, space=None, grant=24):
    def call(*operands):
        specs = [
            pl.BlockSpec(memory_space=space if i < first else pltpu.VMEM)
            for i in range(len(operands))
        ]
        moved = sum(x.size * x.dtype.itemsize for x in operands)
        return pl.pallas_call(
            body,
            out_shape=outs,
            in_specs=specs,
            out_specs=jax.tree.map(lambda _: pl.BlockSpec(memory_space=pltpu.VMEM), outs),
            scratch_shapes=scratch,
            compiler_params=pltpu.CompilerParams(vmem_limit_bytes=grant << 20),
            cost_estimate=pl.CostEstimate(flops=flops, bytes_accessed=moved, transcendentals=0),
        )(*operands)

    return call


def exchange(x, axis):
    return lax.all_to_all(x, axis, split_axis=0, concat_axis=0, tiled=True)


def share(keep, send, back, core):
    half = keep.shape[1]
    tile = 8
    chips = lax.axis_size("graph_0") * lax.axis_size("graph_1")
    samples = lax.axis_size("sample")
    lanes = 2 * half + half // 2
    other = lax.ppermute(send, "graph_2", [(0, 1), (1, 0)])
    packed = kernel(pack, shape((chips, 2, tile, lanes), BF16), [], 10**7)(
        keep.reshape(chips, -1, half),
        other.reshape(chips, -1, half),
        back.reshape(chips, 2, tile, half),
    )
    arrived = exchange(packed.reshape(2 * chips, tile, lanes), GRAPH)
    arrived, core = lax.optimization_barrier((arrived, core))
    copies = kernel(add_chips, shape((samples, 2, tile, lanes - half), F32), [], 10**7)(
        arrived.reshape(chips, 2, tile, lanes)
    )
    copies = exchange(copies, "sample")
    rows = keep.shape[0] // (2 * chips)
    grad_weights = kernel(add_samples, shape((rows, 2 * half), F32), [], 10**6, 1, pltpu.SMEM)(
        1 - core, copies
    )
    return arrived.reshape(2 * chips * tile, lanes), grad_weights


def on_device(
    grid_in,
    mesh_init,
    g2m_geometry,
    w_embed,
    w_g2m,
    w_geo,
    a_send,
    a_recv,
    b_node,
    cotangent,
    g2m_send_rows,
    g2m_counts,
    g2m_senders,
    g2m_receivers,
    mesh_send_rows,
    mesh_senders,
    mesh_receivers,
):
    groups, slots = g2m_send_rows.shape[1:]
    halo_slots = mesh_send_rows.shape[2]
    features = grid_in.shape[2]
    width = w_g2m.shape[1]
    half = width // 2
    nodes = mesh_init.shape[1]
    table_rows = groups * halo_slots + nodes
    halves = 2 * groups * halo_slots

    core = lax.axis_index("graph_2").astype(jnp.int32)[None]
    core, g2m_counts = lax.optimization_barrier((core, g2m_counts))
    grid_rows = jnp.transpose(g2m_send_rows, (0, 2, 1))
    mesh_rows = jnp.transpose(mesh_send_rows, (0, 2, 1))
    raw_rows = kernel(
        pick_grid,
        shape((groups * slots, features), BF16),
        [
            pltpu.VMEM(grid_rows.shape, jnp.int32),
            pltpu.VMEM(g2m_counts.shape, jnp.int32),
            pltpu.VMEM(grid_in.shape, BF16),
            pltpu.SemaphoreType.DMA((3,)),
            pltpu.VMEM((features // LANES, groups * slots, LANES), F32),
        ],
        10**8,
        3,
        pltpu.HBM,
        GRANTS[0],
    )(grid_rows, g2m_counts, grid_in)
    pieces = exchange(raw_rows.reshape(groups, slots, features), GRAPH)

    latent, halo = kernel(
        encode,
        (shape((nodes, width), BF16), shape((halves, half), BF16)),
        [pltpu.VMEM((half // LANES, halves, LANES), F32)],
        2 * 10**9,
        grant=GRANTS[1],
    )(
        pieces.reshape(groups * slots, features),
        g2m_senders[None],
        g2m_receivers[None],
        g2m_geometry,
        w_embed,
        w_g2m,
        w_geo,
        mesh_init,
        mesh_rows,
    )
    halo = exchange(halo.reshape(groups, 2 * halo_slots, half), GRAPH)
    halo, core = lax.optimization_barrier((halo, core))
    sibling = 1 - core

    mesh_out, back, table, send_grad, recv_grad, aggregate, d_update = kernel(
        functools.partial(process, halo_slots),
        (
            shape((1, nodes, width), BF16),
            shape((halves, half), BF16),
            shape((table_rows, width), BF16),
            shape((table_rows, width), BF16),
            shape((nodes, width), BF16),
            shape((nodes, width), BF16),
            shape((nodes, width), BF16),
        ),
        [pltpu.VMEM((half // LANES, halves, LANES), F32)],
        3 * 10**9,
        grant=GRANTS[2],
    )(
        halo.reshape(halves, half),
        latent,
        mesh_senders[None],
        mesh_receivers[None],
        a_send,
        a_recv,
        b_node,
        cotangent,
    )

    operands = (table, send_grad, latent, recv_grad, aggregate, d_update)
    send = kernel(functools.partial(weight_grads, False), shape((3 * width, half), BF16), [], 5 * 10**8, 1, pltpu.SMEM)(sibling, *operands)
    keep = kernel(functools.partial(weight_grads, True), shape((3 * width, half), F32), [], 5 * 10**8, 1, pltpu.SMEM)(sibling, *operands)
    arrived, grad_weights = share(keep, send, back, core)

    grad_mesh = kernel(
        return_grads,
        shape((1, nodes, width), F32),
        [pltpu.VMEM((half // LANES, halves, LANES), F32)],
        10**9,
    )(
        arrived,
        mesh_rows,
        send_grad,
        recv_grad,
        a_send,
        a_recv,
        cotangent,
    )
    return (mesh_out, grad_mesh, grad_weights)


def solution(mesh):
    torus = Mesh(
        mesh.devices.reshape(8, 8, 2, mesh.shape["sample"]),
        ("graph_0", "graph_1", "graph_2", "sample"),
    )
    in_specs = (
        P("sample", GRAPH, None),
        P("sample", GRAPH, None),
        P(None, GRAPH),
        P(),
        P(),
        P(),
        P(),
        P(),
        P(),
        P("sample", GRAPH, None),
        P(GRAPH, None, None),
        P(GRAPH, None),
        P(GRAPH),
        P(GRAPH),
        P(GRAPH, None, None),
        P(GRAPH),
        P(GRAPH),
    )
    out_specs = (P("sample", GRAPH, None), P("sample", GRAPH, None), P(GRAPH, None))
    return jax.shard_map(
        on_device, mesh=torus, in_specs=in_specs, out_specs=out_specs, check_vma=False
    )
```

```python
import functools

import jax
import jax.numpy as jnp
from jax import lax
from jax.experimental import pallas as pl
from jax.experimental.pallas import tpu as pltpu
from jax.sharding import Mesh
from jax.sharding import PartitionSpec as P

GRAPH = ("graph_0", "graph_1", "graph_2")
LANES = 128
F32 = jnp.float32
BF16 = jnp.bfloat16
GRANTS = (60, 40, 40)


def dot(left, right):
    return jnp.dot(left, right, preferred_element_type=F32)


def times_transposed(left, right):
    return lax.dot_general(left, right, (((1,), (1,)), ((), ())), preferred_element_type=F32)


def inner_rows(left, right):
    return lax.dot_general(left, right, (((0,), (0,)), ((), ())), preferred_element_type=F32)


def logistic(v):
    return 1.0 / (1.0 + jnp.exp(-v))


def silu(v):
    return v * logistic(v)


def slope_from(v, s):
    return s * (1.0 + v * (1.0 - s))


def columns_of(row):
    return jnp.transpose(jnp.broadcast_to(row, (LANES, row.shape[1])))


def slot_columns(ids):
    slots, groups = ids.shape
    turned = jnp.transpose(jnp.concatenate([ids] * (LANES // slots), axis=0))
    return [jnp.broadcast_to(turned[:, j : j + 1], (groups, LANES)) for j in range(slots)]


def select_rows(column, size):
    lane = lax.broadcasted_iota(jnp.int32, column.shape, 1)
    blocks = [
        jnp.where(column == lane + LANES * k, 1.0, 0.0).astype(BF16) for k in range(size // LANES)
    ]
    return blocks[0] if len(blocks) == 1 else jnp.concatenate(blocks, axis=1)


def select_columns(row, size):
    segment = lax.broadcasted_iota(jnp.int32, (size, row.shape[1]), 0)
    return jnp.where(segment == row, 1.0, 0.0).astype(BF16)


def strided_store(spread, start, stride, value):
    rows, width = value.shape
    for k in range(width // LANES):
        spread[k, pl.ds(start, rows, stride=stride), :] = value[:, k * LANES : (k + 1) * LANES]


def gather_blocks(spread, out_ref):
    for k in range(spread.shape[0]):
        out_ref[:, k * LANES : (k + 1) * LANES] = spread[k].astype(out_ref.dtype)


def scatter_blocks(spread, in_ref):
    for k in range(spread.shape[0]):
        spread[k] = in_ref[:, k * LANES : (k + 1) * LANES].astype(spread.dtype)


def pick_grid(rows_hbm, counts_hbm, grid_hbm, out_ref, rows, counts, grid, sems, spread):
    copies = [
        pltpu.make_async_copy(source, target, sems.at[i])
        for i, (source, target) in enumerate(
            ((rows_hbm, rows), (counts_hbm, counts), (grid_hbm, grid))
        )
    ]
    for copy in copies:
        copy.start()
    copies[0].wait()
    copies[1].wait()
    slots = rows.shape[1]
    slot = lax.broadcasted_iota(jnp.int32, rows.shape[1:], 0)
    ids = slot_columns(jnp.where(slot < counts[...], rows[0], -1))
    chosen = jnp.concatenate([select_rows(column, grid.shape[1]) for column in ids], axis=0)
    copies[2].wait()
    picked = dot(chosen, grid[0])
    groups = rows.shape[2]
    for j in range(slots):
        strided_store(spread, j, slots, picked[j * groups : (j + 1) * groups])
    gather_blocks(spread, out_ref)


def encode(
    pieces_ref, senders_ref, receivers_ref, geometry_ref, w_embed_ref, w_g2m_ref, w_geo_ref,
    init_ref, send_rows_ref, latent_ref, halo_ref, spread,
):
    edges = senders_ref.shape[1]
    nodes, width = latent_ref.shape
    inputs = geometry_ref.shape[0]
    geometry = geometry_ref[...].astype(F32)
    blank = jnp.zeros((LANES - inputs, edges), F32)
    geometry = jnp.transpose(jnp.concatenate([geometry, blank], axis=0)).astype(BF16)
    blank = jnp.zeros((LANES - inputs, width), F32)
    weights = [w_g2m_ref[...].astype(F32), w_geo_ref[...].astype(F32), blank]
    weights = jnp.concatenate(weights, axis=0).astype(BF16)
    chosen = select_rows(columns_of(senders_ref[...]), pieces_ref.shape[0])
    raw = dot(chosen, pieces_ref[...]).astype(BF16)
    embedded = silu(dot(raw, w_embed_ref[...])).astype(BF16)
    message = silu(dot(jnp.concatenate([embedded, geometry], axis=1), weights)).astype(BF16)
    gather = select_columns(receivers_ref[...], nodes)
    total = init_ref[0].astype(F32) + dot(gather, message)
    latent = total.astype(BF16)
    latent_ref[...] = latent
    ids = slot_columns(send_rows_ref[0])
    picked = dot(jnp.concatenate([select_rows(column, nodes) for column in ids], axis=0), latent)
    groups = send_rows_ref.shape[2]
    for j in range(len(ids)):
        split_store(spread, j, len(ids), picked[j * groups : (j + 1) * groups])
    gather_blocks(spread, halo_ref)


def split_store(spread, j, slots, value):
    groups, width = value.shape
    strided_store(spread, j, 2 * slots, value[:, : width // 2])
    strided_store(spread, slots + j, 2 * slots, value[:, width // 2 :])


def split_load(spread, j, slots, groups):
    blocks = [
        spread[k, pl.ds(start, groups, stride=2 * slots), :]
        for start in (j, slots + j)
        for k in range(spread.shape[0])
    ]
    return jnp.concatenate(blocks, axis=1)


def weight_grads(
    mine, sibling_ref, table_ref, send_grad_ref, latent_ref, recv_grad_ref, aggregate_ref,
    d_update_ref, out_ref,
):
    half = out_ref.shape[1]
    width = latent_ref.shape[1]
    core = 1 - sibling_ref[0] if mine else sibling_ref[0]
    columns = pl.ds(pl.multiple_of(core * half, half), half)
    pairs = ((table_ref, send_grad_ref), (latent_ref, recv_grad_ref), (aggregate_ref, d_update_ref))
    for i, (left, right) in enumerate(pairs):
        product = inner_rows(left[...], right[:, columns])
        out_ref[i * width : (i + 1) * width, :] = product.astype(out_ref.dtype)


def process(
    slots, sibling_ref, halo_ref, latent_ref, senders_ref, receivers_ref, a_send_ref, a_recv_ref, b_node_ref,
    cot_ref,
    out_ref, back_ref, table_ref, send_grad_ref, recv_grad_ref, aggregate_ref, d_update_ref, send_ref,
    spread,
):
    nodes, width = latent_ref.shape
    rows = table_ref.shape[0]
    remote = rows - nodes
    groups = remote // slots
    scatter_blocks(spread, halo_ref)
    for j in range(slots):
        table_ref[j * groups : (j + 1) * groups, :] = split_load(spread, j, slots, groups).astype(BF16)
    latent = latent_ref[...]
    table_ref[remote:, :] = latent
    ids = senders_ref[...]
    ids = jnp.where(ids < remote, lax.rem(ids, slots) * groups + lax.div(ids, slots), ids)
    receivers = receivers_ref[...]
    receive = select_rows(columns_of(receivers), nodes)
    gather = select_columns(receivers, nodes)
    sent = dot(select_rows(columns_of(ids), rows), table_ref[...]).astype(BF16)
    own = dot(receive, latent).astype(BF16)
    weights = jnp.concatenate([a_send_ref[...], a_recv_ref[...]], axis=0)
    pre_act = dot(jnp.concatenate([sent, own], axis=1), weights)
    gate = logistic(pre_act)
    aggregate = dot(gather, (pre_act * gate).astype(BF16)).astype(BF16)
    aggregate_ref[...] = aggregate
    update = dot(aggregate, b_node_ref[...])
    update_gate = logistic(update)
    out_ref[0] = (latent.astype(F32) + update * update_gate).astype(BF16)
    d_update = (cot_ref[0].astype(F32) * slope_from(update, update_gate)).astype(BF16)
    d_update_ref[...] = d_update
    d_aggregate = times_transposed(d_update, b_node_ref[...]).astype(BF16)
    d_pre = (dot(receive, d_aggregate) * slope_from(pre_act, gate)).astype(BF16)
    sums = dot(jnp.concatenate([select_columns(ids, rows), gather], axis=0), d_pre)
    recv_grad_ref[...] = sums[rows:].astype(BF16)
    send_grad = sums[:rows]
    send_grad_ref[...] = send_grad.astype(BF16)
    for j in range(slots):
        split_store(spread, j, slots, send_grad[j * groups : (j + 1) * groups])
    gather_blocks(spread, back_ref)
    weight_grads(
        False, sibling_ref, table_ref, send_grad_ref, latent_ref, recv_grad_ref, aggregate_ref,
        d_update_ref, send_ref,
    )


def keep_grads(
    sibling_ref, table_ref, send_grad_ref, latent_ref, recv_grad_ref, aggregate_ref, d_update_ref,
    a_send_ref, a_recv_ref, cot_ref, keep_ref, local_ref,
):
    weight_grads(
        True, sibling_ref, table_ref, send_grad_ref, latent_ref, recv_grad_ref, aggregate_ref,
        d_update_ref, keep_ref,
    )
    nodes = latent_ref.shape[0]
    own_rows = send_grad_ref[send_grad_ref.shape[0] - nodes :, :]
    local_ref[...] = (
        cot_ref[0].astype(F32)
        + times_transposed(recv_grad_ref[...], a_recv_ref[...])
        + times_transposed(own_rows, a_send_ref[...])
    )


def pack(keep_ref, other_ref, back_ref, out_ref):
    chips, _, half = keep_ref.shape
    tile = back_ref.shape[2]
    out_ref[:, :, :, :half] = back_ref[...]
    for i in range(3):
        rows = slice(i * tile, (i + 1) * tile)
        total = keep_ref[:, rows, :] + other_ref[:, rows, :].astype(F32)
        if i != 1:
            out_ref[:, i // 2, :, half : 2 * half] = total.astype(BF16)
            continue
        flat = total.reshape(chips * tile, half)
        left, right = flat[:, :LANES], flat[:, LANES:]
        upper = lax.rem(lax.broadcasted_iota(jnp.int32, left.shape, 0), tile) < tile // 2
        first = jnp.where(upper, left, pltpu.roll(right, tile // 2, 0))
        second = jnp.where(upper, pltpu.roll(left, chips * tile - tile // 2, 0), right)
        out_ref[:, 0, :, 2 * half :] = first.astype(BF16).reshape(chips, tile, LANES)
        out_ref[:, 1, :, 2 * half :] = second.astype(BF16).reshape(chips, tile, LANES)


def add_chips(arrived_ref, out_ref):
    chips = arrived_ref.shape[0]
    skip = arrived_ref.shape[3] - out_ref.shape[3]
    total = arrived_ref[0, :, :, skip:].astype(F32)
    for i in range(1, chips):
        total = total + arrived_ref[i, :, :, skip:].astype(F32)
    for i in range(out_ref.shape[0]):
        out_ref[i] = total


def add_samples(sibling_ref, arrived_ref, out_ref):
    total = arrived_ref[0]
    for i in range(1, arrived_ref.shape[0]):
        total = total + arrived_ref[i]
    tile = total.shape[1]
    half = out_ref.shape[1] // 2
    extra = tile // 2
    whole = jnp.concatenate([total[h, :, :half] for h in range(2)], axis=1)
    parts = [total[h, k * extra : (k + 1) * extra, half:] for h in range(2) for k in range(2)]
    middle = jnp.concatenate(parts, axis=1)

    @pl.when(sibling_ref[0] == 1)
    def _():
        out_ref[:tile, :] = whole
        out_ref[tile:, :] = middle

    @pl.when(sibling_ref[0] == 0)
    def _():
        out_ref[:extra, :] = middle
        out_ref[extra:, :] = whole


def return_grads(back_ref, send_rows_ref, a_send_ref, local_ref, out_ref, spread):
    nodes = local_ref.shape[0]
    slots, groups = send_rows_ref.shape[1:]
    scatter_blocks(spread, back_ref)
    wanted = send_rows_ref[0]
    arrived = [split_load(spread, j, slots, groups).astype(BF16) for j in range(slots)]
    chosen = [select_columns(wanted[j : j + 1], nodes) for j in range(slots)]
    total = dot(jnp.concatenate(chosen, axis=1), jnp.concatenate(arrived, axis=0))
    high = total.astype(BF16)
    rest = total - high.astype(F32)
    low = rest.astype(BF16)
    a_send = a_send_ref[...]
    out_ref[0] = local_ref[...] + (times_transposed(high, a_send) + times_transposed(low, a_send))


def shape(dims, dtype):
    return jax.ShapeDtypeStruct(dims, dtype)


def kernel(body, outs, scratch, flops, first=0, space=None, grant=24):
    def call(*operands):
        specs = [
            pl.BlockSpec(memory_space=space if i < first else pltpu.VMEM)
            for i in range(len(operands))
        ]
        moved = sum(x.size * x.dtype.itemsize for x in operands)
        return pl.pallas_call(
            body,
            out_shape=outs,
            in_specs=specs,
            out_specs=jax.tree.map(lambda _: pl.BlockSpec(memory_space=pltpu.VMEM), outs),
            scratch_shapes=scratch,
            compiler_params=pltpu.CompilerParams(vmem_limit_bytes=grant << 20),
            cost_estimate=pl.CostEstimate(flops=flops, bytes_accessed=moved, transcendentals=0),
        )(*operands)

    return call


def exchange(x, axis):
    return lax.all_to_all(x, axis, split_axis=0, concat_axis=0, tiled=True)


def share(keep, send, back, core):
    half = keep.shape[1]
    tile = 8
    chips = lax.axis_size("graph_0") * lax.axis_size("graph_1")
    samples = lax.axis_size("sample")
    lanes = 2 * half + half // 2
    other = lax.ppermute(send, "graph_2", [(0, 1), (1, 0)])
    packed = kernel(pack, shape((chips, 2, tile, lanes), BF16), [], 10**7)(
        keep.reshape(chips, -1, half),
        other.reshape(chips, -1, half),
        back.reshape(chips, 2, tile, half),
    )
    arrived = exchange(packed.reshape(2 * chips, tile, lanes), GRAPH)
    copies = kernel(add_chips, shape((samples, 2, tile, lanes - half), F32), [], 10**7)(
        arrived.reshape(chips, 2, tile, lanes)
    )
    copies = exchange(copies, "sample")
    copies, core = lax.optimization_barrier((copies, core))
    return arrived.reshape(2 * chips * tile, lanes), copies, 1 - core


def on_device(
    grid_in,
    mesh_init,
    g2m_geometry,
    w_embed,
    w_g2m,
    w_geo,
    a_send,
    a_recv,
    b_node,
    cotangent,
    g2m_send_rows,
    g2m_counts,
    g2m_senders,
    g2m_receivers,
    mesh_send_rows,
    mesh_senders,
    mesh_receivers,
):
    groups, slots = g2m_send_rows.shape[1:]
    halo_slots = mesh_send_rows.shape[2]
    features = grid_in.shape[2]
    width = w_g2m.shape[1]
    half = width // 2
    nodes = mesh_init.shape[1]
    table_rows = groups * halo_slots + nodes
    halves = 2 * groups * halo_slots

    core = lax.axis_index("graph_2").astype(jnp.int32)[None]
    core, g2m_counts = lax.optimization_barrier((core, g2m_counts))
    grid_rows = jnp.transpose(g2m_send_rows, (0, 2, 1))
    mesh_rows = jnp.transpose(mesh_send_rows, (0, 2, 1))
    raw_rows = kernel(
        pick_grid,
        shape((groups * slots, features), BF16),
        [
            pltpu.VMEM(grid_rows.shape, jnp.int32),
            pltpu.VMEM(g2m_counts.shape, jnp.int32),
            pltpu.VMEM(grid_in.shape, BF16),
            pltpu.SemaphoreType.DMA((3,)),
            pltpu.VMEM((features // LANES, groups * slots, LANES), F32),
        ],
        10**8,
        3,
        pltpu.HBM,
        GRANTS[0],
    )(grid_rows, g2m_counts, grid_in)
    pieces = exchange(raw_rows.reshape(groups, slots, features), GRAPH)

    latent, halo = kernel(
        encode,
        (shape((nodes, width), BF16), shape((halves, half), BF16)),
        [pltpu.VMEM((half // LANES, halves, LANES), F32)],
        2 * 10**9,
        grant=GRANTS[1],
    )(
        pieces.reshape(groups * slots, features),
        g2m_senders[None],
        g2m_receivers[None],
        g2m_geometry,
        w_embed,
        w_g2m,
        w_geo,
        mesh_init,
        mesh_rows,
    )
    halo = exchange(halo.reshape(groups, 2 * halo_slots, half), GRAPH)
    halo, core = lax.optimization_barrier((halo, core))
    sibling = 1 - core

    mesh_out, back, table, send_grad, recv_grad, aggregate, d_update, send = kernel(
        functools.partial(process, halo_slots),
        (
            shape((1, nodes, width), BF16),
            shape((halves, half), BF16),
            shape((table_rows, width), BF16),
            shape((table_rows, width), BF16),
            shape((nodes, width), BF16),
            shape((nodes, width), BF16),
            shape((nodes, width), BF16),
            shape((3 * width, half), BF16),
        ),
        [pltpu.VMEM((half // LANES, halves, LANES), F32)],
        3 * 10**9,
        1,
        pltpu.SMEM,
        GRANTS[2],
    )(
        sibling,
        halo.reshape(halves, half),
        latent,
        mesh_senders[None],
        mesh_receivers[None],
        a_send,
        a_recv,
        b_node,
        cotangent,
    )

    operands = (table, send_grad, latent, recv_grad, aggregate, d_update)
    keep, local = kernel(
        keep_grads,
        (shape((3 * width, half), F32), shape((nodes, width), F32)),
        [],
        7 * 10**8,
        1,
        pltpu.SMEM,
    )(sibling, *operands, a_send, a_recv, cotangent)
    arrived, copies, sibling = share(keep, send, back, core)
    grad_weights = kernel(
        add_samples, shape((3 * width // groups, width), F32), [], 10**6, 1, pltpu.SMEM
    )(sibling, copies)
    grad_mesh = kernel(
        return_grads,
        shape((1, nodes, width), F32),
        [pltpu.VMEM((half // LANES, halves, LANES), F32)],
        10**9,
    )(arrived, mesh_rows, a_send, local)
    return (mesh_out, grad_mesh, grad_weights)


def solution(mesh):
    torus = Mesh(
        mesh.devices.reshape(8, 8, 2, mesh.shape["sample"]),
        ("graph_0", "graph_1", "graph_2", "sample"),
    )
    in_specs = (
        P("sample", GRAPH, None),
        P("sample", GRAPH, None),
        P(None, GRAPH),
        P(),
        P(),
        P(),
        P(),
        P(),
        P(),
        P("sample", GRAPH, None),
        P(GRAPH, None, None),
        P(GRAPH, None),
        P(GRAPH),
        P(GRAPH),
        P(GRAPH, None, None),
        P(GRAPH),
        P(GRAPH),
    )
    out_specs = (P("sample", GRAPH, None), P("sample", GRAPH, None), P(GRAPH, None))
    return jax.shard_map(
        on_device, mesh=torus, in_specs=in_specs, out_specs=out_specs, check_vma=False
    )
```
